512 devices in a mesh: dp: 2 (over z_hi), row: 8 (over y, core), col: 32 (over x, z_lo).
Axes of the slice: x: 4, y: 4, z: 16 (z_hi: 2, z_lo: 8; z = z_hi * 8 + z_lo), core: 2. Of those that a mesh axis runs over, the one named last changes fastest.
Arguments:
- activations: bfloat16 [2048, 16384], P(('dp', 'row'), 'col'), may hold values from -6 to 6
- cotangent: bfloat16 [2048, 16384], P(('dp', 'row'), 'col'), may hold values from -6 to 6
- gate_saved: bfloat16 [2048, 6656], P(('dp', 'col'), 'row'), may hold values from -6 to 6
- up_saved: bfloat16 [2048, 6656], P(('dp', 'col'), 'row'), may hold values from -6 to 6
- w_gate: bfloat16 [16384, 6656], P('col', 'row'), may hold values from -0.046875 to 0.046875
- w_up: bfloat16 [16384, 6656], P('col', 'row'), may hold values from -0.046875 to 0.046875
- w_down: bfloat16 [6656, 16384], P('row', 'col'), may hold values from -0.078125 to 0.078125
- assignment: int32 [4], replicated, may hold values from 0 to 3, each once
- pair_lengths: int32 [8], replicated, may hold values from 1 to 256, 1536 in all
Outputs:
- input_grad: bfloat16 [2048, 16384], P(('dp', 'row'), 'col')
- gate_grad: bfloat16 [16384, 6656], P(('col', 'dp'), 'row')
- up_grad: bfloat16 [16384, 6656], P(('col', 'dp'), 'row')
- down_grad: bfloat16 [6656, 16384], P(('row', 'dp'), 'col')
The draws below stay inside these ranges and needn't reach their ends.
Inputs may be any that keep to these rules, and one draw needn't show every extreme that they name: `assignment`: each of the 4 pairs stands in exactly one pair slot; pair slot s belongs to batch s // 2. `pair_lengths`: entry 2 p is the live length of pair p's chosen sequence and entry 2 p + 1 that of its rejected one; the largest entry is exactly 256.
All inputs are finite; a program needn't handle non-finite values.
Results may differ from the reference program's by a relative error of at most 0.019.
Values may be sent and summed in bfloat16 or wider, within the bound.
No kernel may reach another device: no remote copies, remote signals or barrier semaphores. Data moves between devices by JAX's collectives and lax.ppermute only.
A program may use at most 64 MiB of HBM per device.

```python
import math
import jax
import jax.numpy as jnp
import numpy as np
from jax import lax

D = 16384
FF = 6656
SEQ = 256
TOK = 1024
PAIRS = 4
TOKENS = 2048
N_DP = 2
N_ROW = 8
N_COL = 32


def raised(array, rng, source, target, shards_of, factor):
    def block_of(dim):
        return (jnp.arange(array.shape[dim]) // (array.shape[dim] // shards_of)).reshape((-1,) + (1,) * (array.ndim - 1 - dim))

    first = jax.random.permutation(rng, shards_of)[block_of(target)]
    other_side = (block_of(target) + shards_of // 2) % shards_of
    return jnp.where((block_of(source) == first) | (block_of(source) == other_side), factor * array, array)


def shard_levels(stream_key, extent, cuts, least, largest):
    loudness = 1.0
    for dim, shards_of in cuts:
        draws = jax.random.uniform(jax.random.fold_in(jax.random.fold_in(stream_key, 6), dim), (shards_of,), jnp.float32, least / len(cuts), largest / len(cuts))
        loudness = loudness * jnp.repeat(jnp.exp(draws), extent[dim] // shards_of).reshape((-1,) + (1,) * (len(extent) - 1 - dim))
    return loudness


def profile(amount, total, limit, skew):
    weights = [(1 << 20) // math.isqrt(rank ** skew) + 1 for rank in range(2, amount + 1)]
    surplus, counts = total - limit - (amount - 1), [1] * (amount - 1)
    while surplus > 0:
        movable = [i for i in range(amount - 1) if counts[i] < limit]
        mass, budget = sum([weights[i] for i in movable]), surplus
        for i in movable:
            addition = min(limit - counts[i], max(1, budget * weights[i] // mass), surplus)
            counts[i] = counts[i] + addition
            surplus = surplus - addition
    return np.array([limit] + counts)


def ragged_sizes(stream_key, count, total, most, slope):
    if count == 2:
        one = jax.random.randint(stream_key, (), max(1, total - most), min(most, total - 1) + 1)
        return jnp.stack([one, total - one])
    lengths = jnp.asarray(profile(count, total, most, slope), jnp.int32)
    twos = (count - 1) // 2
    source_of, receiver = lengths[1:1 + 2 * twos:2], lengths[2:2 + 2 * twos:2]
    slack = jnp.minimum(source_of - 1, most - receiver)
    moved = jax.random.randint(jax.random.fold_in(stream_key, 1), (twos,), 0, 1 << 20) % (slack + 1)
    lengths = lengths.at[1:1 + 2 * twos:2].set(source_of - moved).at[2:2 + 2 * twos:2].set(receiver + moved)
    return lengths[jax.random.permutation(jax.random.fold_in(stream_key, 2), count)]


def gaussian(stream_key, shape, width, bound, pieces=(), kind=jnp.bfloat16):
    result = width * jax.random.normal(stream_key, shape, jnp.float32)
    if pieces:
        result = result * shard_levels(stream_key, shape, pieces, -0.22, 0.18)
    return jnp.clip(result, -bound, bound).astype(kind)


def bell_draw_with(key, dims, width, reach, pieces, heavy, kind=jnp.bfloat16):
    values = width * jax.random.normal(key, dims, jnp.float32)
    if pieces:
        values = values * shard_levels(key, dims, pieces, -0.22, 0.18)
    return jnp.clip(raised(values, jax.random.fold_in(key, 3), *heavy), -reach, reach).astype(kind)


def setup_inputs(seed: int = 0) -> dict:
    arg_keys = jax.random.split(jax.random.key(seed), 10)
    activations = bell_draw_with(arg_keys[0], (TOKENS, D), 1.0, 6.0, ((0, 16), (1, 32)), (0, 1, 32, 2.75))
    cotangent = bell_draw_with(arg_keys[1], (TOKENS, D), 1.0, 6.0, ((0, 16), (1, 32)), (1, 0, 32, 2.75))
    gate_saved = gaussian(arg_keys[2], (TOKENS, FF), 1.0, 6.0, ((0, 64), (1, 8)))
    up_saved = gaussian(arg_keys[3], (TOKENS, FF), 1.0, 6.0, ((0, 64), (1, 8)))
    w_gate = gaussian(arg_keys[4], (D, FF), D ** -0.5, 0.046875, ((0, 32), (1, 8)))
    w_up = gaussian(arg_keys[5], (D, FF), D ** -0.5, 0.046875, ((0, 32), (1, 8)))
    w_down = gaussian(arg_keys[6], (FF, D), FF ** -0.5, 0.078125, ((0, 8), (1, 32)))
    assignment = jax.random.permutation(arg_keys[7], PAIRS).astype(jnp.int32)
    pair_lengths = ragged_sizes(arg_keys[8], 2 * PAIRS, 3 * PAIRS * SEQ // 2, SEQ, 1).astype(jnp.int32)
    return dict(activations=activations, cotangent=cotangent, gate_saved=gate_saved, up_saved=up_saved, w_gate=w_gate, w_up=w_up, w_down=w_down, assignment=assignment, pair_lengths=pair_lengths)


def round_trip(values):
    return lax.optimization_barrier(values.astype(jnp.bfloat16)).astype(jnp.float32)

def contract_last(left, right):
    return lax.dot_general(left, right, (((1,), (1,)), ((), ())), preferred_element_type=jnp.float32)

def contract_first(left, right):
    return lax.dot_general(left, right, (((0,), (0,)), ((), ())), preferred_element_type=jnp.float32)

def reference(activations, cotangent, gate_saved, up_saved, w_gate, w_up, w_down, assignment, pair_lengths):
    position = jnp.arange(TOKENS, dtype=jnp.int32)
    slot_ids = position // (2 * SEQ)
    pair_ids = assignment[slot_ids]
    entry_ids = 2 * pair_ids + position // SEQ % 2
    live_tokens = position % SEQ < pair_lengths[entry_ids]
    masked = jnp.where(live_tokens[:, None], cotangent, jnp.zeros_like(cotangent))
    col_width = D // N_COL

    def head_block(total, index):
        start = index * col_width
        left = lax.dynamic_slice_in_dim(masked, start, col_width, 1)
        right = lax.dynamic_slice_in_dim(w_down, start, col_width, 1)
        return (total + round_trip(contract_last(left, right)), None)
    head_grad, _ = lax.scan(head_block, jnp.zeros((TOKENS, FF), jnp.float32), jnp.arange(N_COL, dtype=jnp.int32))
    gate_float = gate_saved.astype(jnp.float32)
    up_float = up_saved.astype(jnp.float32)
    sigmoid_gate = jax.nn.sigmoid(gate_float)
    silu_gate = gate_float * sigmoid_gate
    hidden = (silu_gate * up_float).astype(jnp.bfloat16)
    grad_gate = (head_grad * up_float * sigmoid_gate * (1.0 + gate_float * (1.0 - sigmoid_gate))).astype(jnp.bfloat16)
    grad_up = (head_grad * silu_gate).astype(jnp.bfloat16)
    row_width = FF // N_ROW

    def input_block(total, index):
        start = index * row_width
        left_gate = lax.dynamic_slice_in_dim(grad_gate, start, row_width, 1)
        left_up = lax.dynamic_slice_in_dim(grad_up, start, row_width, 1)
        right_gate = lax.dynamic_slice_in_dim(w_gate, start, row_width, 1)
        right_up = lax.dynamic_slice_in_dim(w_up, start, row_width, 1)
        term = contract_last(left_gate, right_gate) + contract_last(left_up, right_up)
        return (total + round_trip(term), None)
    input_sum, _ = lax.scan(input_block, jnp.zeros((TOKENS, D), jnp.float32), jnp.arange(N_ROW, dtype=jnp.int32))
    input_grad = input_sum.astype(jnp.bfloat16)
    grad_scale = 1.0 / jnp.sqrt(jnp.float32(TOKENS))
    gate_total = jnp.zeros((D, FF), jnp.float32)
    up_total = jnp.zeros((D, FF), jnp.float32)
    down_total = jnp.zeros((FF, D), jnp.float32)
    for batch_index in range(N_DP):
        first = batch_index * TOK
        last = first + TOK
        gate_total = gate_total + round_trip(contract_first(activations[first:last], grad_gate[first:last]) * grad_scale)
        up_total = up_total + round_trip(contract_first(activations[first:last], grad_up[first:last]) * grad_scale)
        down_total = down_total + round_trip(contract_first(hidden[first:last], masked[first:last]) * grad_scale)
    return (input_grad, gate_total.astype(jnp.bfloat16), up_total.astype(jnp.bfloat16), down_total.astype(jnp.bfloat16))
```

```python
import jax
import jax.numpy as jnp
from jax import lax
from jax.sharding import Mesh, PartitionSpec as P

SEQ = 256
N_Y, N_CORE, N_X, N_Z = 4, 2, 4, 8


def contract_last(left, right):
    return lax.dot_general(
        left, right, (((1,), (1,)), ((), ())), preferred_element_type=jnp.float32
    )


def contract_first(left, right):
    return lax.dot_general(
        left, right, (((0,), (0,)), ((), ())), preferred_element_type=jnp.float32
    )


def live_mask(assignment, pair_lengths, row_count):
    seq_count = row_count // SEQ
    seq_index = jnp.arange(seq_count, dtype=jnp.int32)
    slot_table = jnp.arange(assignment.shape[0], dtype=jnp.int32)
    pair_ids = jnp.sum(
        jnp.where(slot_table[None, :] == seq_index[:, None] // 2, assignment[None, :], 0), axis=1
    )
    entry_ids = 2 * pair_ids + seq_index % 2
    entry_table = jnp.arange(pair_lengths.shape[0], dtype=jnp.int32)
    live_len = jnp.sum(
        jnp.where(entry_table[None, :] == entry_ids[:, None], pair_lengths[None, :], 0), axis=1
    )
    position = jnp.arange(SEQ, dtype=jnp.int32)
    return position[None, :] < live_len[:, None]


def shift(value, axis, size, step):
    return lax.ppermute(value, axis, [(i, (i + step) % size) for i in range(size)])


def spread(value, axis, size):
    copies = jnp.broadcast_to(value[None], (size,) + value.shape)
    return lax.all_to_all(copies, axis, split_axis=0, concat_axis=0, tiled=True)


def sum_over(value, axis, size):
    blocks = value.reshape(size, value.shape[0] // size, value.shape[1])
    received = lax.all_to_all(blocks, axis, split_axis=0, concat_axis=0, tiled=True)
    return jnp.sum(received, axis=0, dtype=jnp.float32).astype(jnp.bfloat16)


def gather_x(block):
    x = lax.axis_index("x")
    half = block.shape[0] // 2
    left = shift(block, "x", N_X, 1)
    right = shift(block, "x", N_X, -1)
    far_low = shift(left[:half], "x", N_X, 1)
    far_high = shift(right[half:], "x", N_X, -1)
    far = jnp.concatenate([far_low, far_high], axis=0)
    out = jnp.zeros((N_X,) + block.shape, block.dtype)
    for step, part in ((0, block), (N_X - 1, left), (1, right), (2, far)):
        out = lax.dynamic_update_slice_in_dim(out, part[None], (x + step) % N_X, 0)
    return out


def on_device(
    activations, cotangent, gate_saved, up_saved, w_gate, w_up, w_down, assignment, pair_lengths
):
    batch = lax.axis_index("dp")
    rows, width = cotangent.shape
    half = width // 2
    own, ffw = gate_saved.shape
    row_axes = ("y", "core")
    n_row = N_Y * N_CORE
    tok = rows * n_row
    n_dp = 2

    saved = jnp.stack([gate_saved, up_saved])[None]
    saved = lax.all_gather(saved, ("dp", "z"), axis=0, tiled=True)
    saved = lax.all_gather(saved, "x", axis=0, tiled=True)
    saved = saved.reshape(N_X, n_dp, N_Z, 2, own, ffw)

    act_own = lax.dynamic_slice_in_dim(activations, batch * half, half, 1)
    act_other = lax.dynamic_slice_in_dim(activations, (1 - batch) * half, half, 1)
    partner = shift(jnp.concatenate([cotangent, act_other], axis=1), "dp", n_dp, 1)

    live = live_mask(assignment, pair_lengths, n_dp * tok).reshape(n_dp, tok)
    live_own = lax.dynamic_index_in_dim(live, batch, 0, keepdims=False)
    live_away = lax.dynamic_index_in_dim(live, 1 - batch, 0, keepdims=False)

    cot_own = spread(cotangent, row_axes, n_row).reshape(tok, width)
    zero = jnp.zeros((), cotangent.dtype)
    masked_own = jnp.where(live_own[:, None], cot_own, zero)
    block_term = contract_last(masked_own, w_down).astype(jnp.bfloat16)
    head = sum_over(block_term, "x", N_X)
    head, partner = lax.optimization_barrier((head, partner))
    head = sum_over(head, "z", N_Z)
    head = lax.all_gather(head, ("dp", "z"), axis=0, tiled=True)
    head = gather_x(head).reshape(N_X, n_dp, N_Z, own, ffw)

    rest = jnp.concatenate([partner, act_own], axis=1)
    rest = lax.all_gather(rest, row_axes, axis=0, tiled=True)
    masked_away = jnp.where(live_away[:, None], rest[:, :width], zero)
    act_away = rest[:, width : width + half]
    act_here = rest[:, width + half :]

    head_f = head.astype(jnp.float32)
    gate = saved[:, :, :, 0].astype(jnp.float32)
    up = saved[:, :, :, 1].astype(jnp.float32)
    sig = jax.nn.sigmoid(gate)
    silu = gate * sig
    hidden = (silu * up).astype(jnp.bfloat16)
    grad_gate = (head_f * up * sig * (1.0 + gate * (1.0 - sig))).astype(jnp.bfloat16)
    grad_up = (head_f * silu).astype(jnp.bfloat16)

    def of_batch(value, index):
        part = lax.dynamic_index_in_dim(value, index, 1, keepdims=False)
        return part.reshape(tok, ffw)

    gg_own, gg_away = of_batch(grad_gate, batch), of_batch(grad_gate, 1 - batch)
    gu_own, gu_away = of_batch(grad_up, batch), of_batch(grad_up, 1 - batch)
    f_half = ffw // 2
    hid_own = lax.dynamic_slice_in_dim(of_batch(hidden, batch), batch * f_half, f_half, 1)
    hid_away = lax.dynamic_slice_in_dim(of_batch(hidden, 1 - batch), batch * f_half, f_half, 1)

    term = (contract_last(gg_own, w_gate) + contract_last(gu_own, w_up)).astype(jnp.bfloat16)
    input_grad = sum_over(term, row_axes, n_row)

    scale = 1.0 / jnp.sqrt(jnp.float32(n_dp * tok))
    gate_grad = (contract_first(act_here, gg_own) + contract_first(act_away, gg_away)) * scale
    up_grad = (contract_first(act_here, gu_own) + contract_first(act_away, gu_away)) * scale
    down_grad = (contract_first(hid_own, masked_own) + contract_first(hid_away, masked_away)) * scale
    return (
        input_grad,
        gate_grad.astype(jnp.bfloat16),
        up_grad.astype(jnp.bfloat16),
        down_grad.astype(jnp.bfloat16),
    )


def solution(mesh):
    fine = Mesh(
        mesh.devices.reshape(2, N_Y, N_CORE, N_X, N_Z), ("dp", "y", "core", "x", "z")
    )
    row, col = ("y", "core"), ("x", "z")
    return jax.shard_map(
        on_device,
        mesh=fine,
        in_specs=(
            P(("dp",) + row, col),
            P(("dp",) + row, col),
            P(("dp",) + col, row),
            P(("dp",) + col, row),
            P(col, row),
            P(col, row),
            P(row, col),
            P(),
            P(),
        ),
        out_specs=(
            P(("dp",) + row, col),
            P(col + ("dp",), row),
            P(col + ("dp",), row),
            P(row + ("dp",), col),
        ),
        check_vma=False,
    )
```

```python
import jax
import jax.numpy as jnp
from jax import lax
from jax.sharding import Mesh, PartitionSpec as P

SEQ = 256
N_Y, N_CORE, N_X, N_Z = 4, 2, 4, 8


def contract_last(left, right):
    return lax.dot_general(
        left, right, (((1,), (1,)), ((), ())), preferred_element_type=jnp.float32
    )


def contract_first(left, right):
    return lax.dot_general(
        left, right, (((0,), (0,)), ((), ())), preferred_element_type=jnp.float32
    )


def live_mask(assignment, pair_lengths, row_count):
    seq_count = row_count // SEQ
    seq_index = jnp.arange(seq_count, dtype=jnp.int32)
    slot_table = jnp.arange(assignment.shape[0], dtype=jnp.int32)
    pair_ids = jnp.sum(
        jnp.where(slot_table[None, :] == seq_index[:, None] // 2, assignment[None, :], 0), axis=1
    )
    entry_ids = 2 * pair_ids + seq_index % 2
    entry_table = jnp.arange(pair_lengths.shape[0], dtype=jnp.int32)
    live_len = jnp.sum(
        jnp.where(entry_table[None, :] == entry_ids[:, None], pair_lengths[None, :], 0), axis=1
    )
    position = jnp.arange(SEQ, dtype=jnp.int32)
    return position[None, :] < live_len[:, None]


def shift(value, axis, size, step):
    return lax.ppermute(value, axis, [(i, (i + step) % size) for i in range(size)])


def spread(value, axis, size):
    copies = jnp.broadcast_to(value[None], (size,) + value.shape)
    return lax.all_to_all(copies, axis, split_axis=0, concat_axis=0, tiled=True)


def sum_over(value, axis, size):
    blocks = value.reshape(size, value.shape[0] // size, value.shape[1])
    received = lax.all_to_all(blocks, axis, split_axis=0, concat_axis=0, tiled=True)
    return jnp.sum(received, axis=0, dtype=jnp.float32).astype(jnp.bfloat16)


def gather_x(block):
    x = lax.axis_index("x")
    left, right = shift(block, "x", N_X, 1), shift(block, "x", N_X, -1)
    far_low, far_high = shift(left[0], "x", N_X, 1), shift(right[1], "x", N_X, -1)
    outs = []
    for side, far in ((0, far_low), (1, far_high)):
        out = jnp.zeros((N_X,) + block.shape[1:], block.dtype)
        for step, part in ((0, block[side]), (N_X - 1, left[side]), (1, right[side]), (2, far)):
            out = lax.dynamic_update_slice_in_dim(out, part[None], (x + step) % N_X, 0)
        outs.append(out)
    return outs


def on_device(
    activations, cotangent, gate_saved, up_saved, w_gate, w_up, w_down, assignment, pair_lengths
):
    batch = lax.axis_index("dp")
    rows, width = cotangent.shape
    half = width // 2
    own, ffw = gate_saved.shape
    row_axes = ("y", "core")
    n_row = N_Y * N_CORE
    tok = rows * n_row
    n_dp = 2
    away = 1 - batch

    def pick(value, index):
        return lax.dynamic_index_in_dim(value, index, 0, keepdims=False)

    act_own = lax.dynamic_slice_in_dim(activations, batch * half, half, 1)
    act_other = lax.dynamic_slice_in_dim(activations, away * half, half, 1)
    partner = shift(jnp.concatenate([cotangent, act_other], axis=1), "dp", n_dp, 1)

    saved = jnp.stack([gate_saved, up_saved])[None]
    saved = lax.all_gather(saved, ("dp", "z"), axis=0, tiled=True)

    live = live_mask(assignment, pair_lengths, n_dp * tok).reshape(n_dp, tok)
    zero = jnp.zeros((), cotangent.dtype)

    cot_own = spread(cotangent, row_axes, n_row).reshape(tok, width)
    masked_own = jnp.where(pick(live, batch)[:, None], cot_own, zero)
    block_term = contract_last(masked_own, w_down).astype(jnp.bfloat16)
    head_x = sum_over(block_term, "x", N_X)
    _, saved, partner = lax.optimization_barrier((head_x, saved, partner))
    saved = saved.reshape(n_dp, N_Z, 2, own, ffw)
    saved_own = pick(saved, batch).transpose(1, 0, 2, 3).reshape(2, N_Z * own, ffw)
    saved_away = pick(saved, away).transpose(1, 0, 2, 3).reshape(2, N_Z * own, ffw)
    saved_own, saved_away = gather_x(jnp.stack([saved_own, saved_away]))

    rest = jnp.concatenate([partner, act_own], axis=1)
    rest = lax.all_gather(rest, row_axes, axis=0, tiled=True)
    masked_away = jnp.where(pick(live, away)[:, None], rest[:, :width], zero)
    act_away = rest[:, width : width + half]
    act_here = rest[:, width + half :]

    def factors(pair):
        gate = pair[:, 0].astype(jnp.float32).reshape(tok, ffw)
        up = pair[:, 1].astype(jnp.float32).reshape(tok, ffw)
        sig = jax.nn.sigmoid(gate)
        silu = gate * sig
        slope = (up * sig * (1.0 + gate * (1.0 - sig))).astype(jnp.bfloat16)
        hidden = (silu * up).astype(jnp.bfloat16)
        return lax.optimization_barrier((slope, silu.astype(jnp.bfloat16), hidden))

    slope_own, silu_own, hid_own = factors(saved_own)
    slope_away, silu_away, hid_away = factors(saved_away)

    head = sum_over(head_x, "z", N_Z)
    head = lax.all_gather(head, ("dp", "z"), axis=0, tiled=True)
    head = head.reshape(n_dp, N_Z * own, ffw)
    head_own, head_away = pick(head, batch), pick(head, away)
    halves = (2, N_Z * own // 2, ffw)
    head_own = jnp.concatenate(gather_x(head_own.reshape(halves)), axis=1)
    head_away = jnp.concatenate(gather_x(head_away.reshape(halves)), axis=1)

    def times(head_rows, factor):
        value = head_rows.reshape(tok, ffw).astype(jnp.float32) * factor.astype(jnp.float32)
        return value.astype(jnp.bfloat16)

    gg_own, gu_own = times(head_own, slope_own), times(head_own, silu_own)
    gg_away, gu_away = times(head_away, slope_away), times(head_away, silu_away)
    term = (contract_last(gg_own, w_gate) + contract_last(gu_own, w_up)).astype(jnp.bfloat16)
    input_grad = sum_over(term, row_axes, n_row)

    scale = 1.0 / jnp.sqrt(jnp.float32(n_dp * tok))
    f_half = ffw // 2
    hid_own = lax.dynamic_slice_in_dim(hid_own, batch * f_half, f_half, 1)
    hid_away = lax.dynamic_slice_in_dim(hid_away, batch * f_half, f_half, 1)
    down_grad = (contract_first(hid_own, masked_own) + contract_first(hid_away, masked_away)) * scale
    gate_grad = (contract_first(act_here, gg_own) + contract_first(act_away, gg_away)) * scale
    up_grad = (contract_first(act_here, gu_own) + contract_first(act_away, gu_away)) * scale
    return (
        input_grad,
        gate_grad.astype(jnp.bfloat16),
        up_grad.astype(jnp.bfloat16),
        down_grad.astype(jnp.bfloat16),
    )


def solution(mesh):
    fine = Mesh(
        mesh.devices.reshape(2, N_Y, N_CORE, N_X, N_Z), ("dp", "y", "core", "x", "z")
    )
    row, col = ("y", "core"), ("x", "z")

    return jax.shard_map(
        on_device,
        mesh=fine,
        in_specs=(
            P(("dp",) + row, col),
            P(("dp",) + row, col),
            P(("dp",) + col, row),
            P(("dp",) + col, row),
            P(col, row),
            P(col, row),
            P(row, col),
            P(),
            P(),
        ),
        out_specs=(
            P(("dp",) + row, col),
            P(col + ("dp",), row),
            P(col + ("dp",), row),
            P(row + ("dp",), col),
        ),
        check_vma=False,
    )
```

```python
import jax
import jax.numpy as jnp
from jax import lax
from jax.sharding import Mesh, PartitionSpec as P

SEQ = 256
N_Y, N_CORE, N_X, N_Z = 4, 2, 4, 8


def contract_last(left, right):
    return lax.dot_general(
        left, right, (((1,), (1,)), ((), ())), preferred_element_type=jnp.float32
    )


def contract_first(left, right):
    return lax.dot_general(
        left, right, (((0,), (0,)), ((), ())), preferred_element_type=jnp.float32
    )


def live_mask(assignment, pair_lengths, row_count):
    seq_count = row_count // SEQ
    seq_index = jnp.arange(seq_count, dtype=jnp.int32)
    slot_table = jnp.arange(assignment.shape[0], dtype=jnp.int32)
    pair_ids = jnp.sum(
        jnp.where(slot_table[None, :] == seq_index[:, None] // 2, assignment[None, :], 0), axis=1
    )
    entry_ids = 2 * pair_ids + seq_index % 2
    entry_table = jnp.arange(pair_lengths.shape[0], dtype=jnp.int32)
    live_len = jnp.sum(
        jnp.where(entry_table[None, :] == entry_ids[:, None], pair_lengths[None, :], 0), axis=1
    )
    position = jnp.arange(SEQ, dtype=jnp.int32)
    return position[None, :] < live_len[:, None]


def shift(value, axis, size, step):
    return lax.ppermute(value, axis, [(i, (i + step) % size) for i in range(size)])


def spread(value, axis, size):
    copies = jnp.broadcast_to(value[None], (size,) + value.shape)
    return lax.all_to_all(copies, axis, split_axis=0, concat_axis=0, tiled=True)


def sum_over(value, axis, size):
    blocks = value.reshape(size, value.shape[0] // size, value.shape[1])
    received = lax.all_to_all(blocks, axis, split_axis=0, concat_axis=0, tiled=True)
    return jnp.sum(received, axis=0, dtype=jnp.float32).astype(jnp.bfloat16)


def gather_x(block):
    x = lax.axis_index("x")
    left, right = shift(block, "x", N_X, 1), shift(block, "x", N_X, -1)
    far = jnp.stack([shift(left[0], "x", N_X, 1), shift(right[1], "x", N_X, -1)])
    out = jnp.zeros((N_X,) + block.shape, block.dtype)
    for step, part in ((0, block), (N_X - 1, left), (1, right), (2, far)):
        out = lax.dynamic_update_slice_in_dim(out, part[None], (x + step) % N_X, 0)
    return out


def on_device(
    activations, cotangent, gate_saved, up_saved, w_gate, w_up, w_down, assignment, pair_lengths
):
    batch = lax.axis_index("dp")
    rows, width = cotangent.shape
    half = width // 2
    own, ffw = gate_saved.shape
    row_axes = ("y", "core")
    n_row = N_Y * N_CORE
    tok = rows * n_row
    n_dp = 2
    away = 1 - batch

    def pick(value, index):
        return lax.dynamic_index_in_dim(value, index, 0, keepdims=False)

    act_own = lax.dynamic_slice_in_dim(activations, batch * half, half, 1)
    act_other = lax.dynamic_slice_in_dim(activations, away * half, half, 1)
    partner = shift(jnp.concatenate([cotangent, act_other], axis=1), "dp", n_dp, 1)

    saved = jnp.stack([gate_saved, up_saved])[None]
    saved = lax.all_gather(saved, ("dp", "z"), axis=0, tiled=True)

    live = live_mask(assignment, pair_lengths, n_dp * tok).reshape(n_dp, tok)
    zero = jnp.zeros((), cotangent.dtype)

    cot_own = spread(cotangent, row_axes, n_row).reshape(tok, width)
    masked_own = jnp.where(pick(live, batch)[:, None], cot_own, zero)
    block_term = contract_last(masked_own, w_down).astype(jnp.bfloat16)
    head_x = sum_over(block_term, "x", N_X)
    _, saved, partner = lax.optimization_barrier((head_x, saved, partner))
    saved = saved.reshape(n_dp, N_Z, 2, own, ffw)
    saved_own, saved_away = pick(saved, batch), pick(saved, away)
    saved_own = lax.all_gather(saved_own, "x", axis=0)
    saved_away = lax.all_gather(saved_away, "x", axis=0)

    rest = spread(jnp.concatenate([partner, act_own], axis=1), row_axes, n_row)
    rest = rest.reshape(tok, 2 * width)
    masked_away = jnp.where(pick(live, away)[:, None], rest[:, :width], zero)
    act_away = rest[:, width : width + half]
    act_here = rest[:, width + half :]

    def factors(pair):
        gate = pair[:, :, 0].astype(jnp.float32).reshape(tok, ffw)
        up = pair[:, :, 1].astype(jnp.float32).reshape(tok, ffw)
        sig = jax.nn.sigmoid(gate)
        silu = gate * sig
        slope = (up * sig * (1.0 + gate * (1.0 - sig))).astype(jnp.bfloat16)
        hidden = (silu * up).astype(jnp.bfloat16)
        return lax.optimization_barrier((slope, silu.astype(jnp.bfloat16), hidden))

    slope_own, silu_own, hid_own = factors(saved_own)
    slope_away, silu_away, hid_away = factors(saved_away)

    head = sum_over(head_x, "z", N_Z)
    head = lax.all_gather(head, ("dp", "z"), axis=0, tiled=True)
    head = head.reshape(n_dp, N_Z * own, ffw)
    head_own = spread(pick(head, batch), "x", N_X)
    halves = (2, N_Z * own // 2, ffw)
    head_away = gather_x(pick(head, away).reshape(halves))

    head_own, head_away = lax.optimization_barrier(head_own), lax.optimization_barrier(head_away)

    def times(head_rows, factor):
        value = head_rows.reshape(tok, ffw).astype(jnp.float32) * factor.astype(jnp.float32)
        return value.astype(jnp.bfloat16)

    gg_own, gu_own = times(head_own, slope_own), times(head_own, silu_own)
    gg_away, gu_away = times(head_away, slope_away), times(head_away, silu_away)
    term = (contract_last(gg_own, w_gate) + contract_last(gu_own, w_up)).astype(jnp.bfloat16)
    input_grad = sum_over(term, row_axes, n_row)

    scale = 1.0 / jnp.sqrt(jnp.float32(n_dp * tok))
    f_half = ffw // 2
    hid_own = lax.dynamic_slice_in_dim(hid_own, batch * f_half, f_half, 1)
    hid_away = lax.dynamic_slice_in_dim(hid_away, batch * f_half, f_half, 1)
    down_grad = (contract_first(hid_own, masked_own) + contract_first(hid_away, masked_away)) * scale
    gate_grad = (contract_first(act_here, gg_own) + contract_first(act_away, gg_away)) * scale
    up_grad = (contract_first(act_here, gu_own) + contract_first(act_away, gu_away)) * scale
    return (
        input_grad,
        gate_grad.astype(jnp.bfloat16),
        up_grad.astype(jnp.bfloat16),
        down_grad.astype(jnp.bfloat16),
    )


def solution(mesh):
    fine = Mesh(
        mesh.devices.reshape(2, N_Y, N_CORE, N_X, N_Z), ("dp", "y", "core", "x", "z")
    )
    row, col = ("y", "core"), ("x", "z")

    return jax.shard_map(
        on_device,
        mesh=fine,
        in_specs=(
            P(("dp",) + row, col),
            P(("dp",) + row, col),
            P(("dp",) + col, row),
            P(("dp",) + col, row),
            P(col, row),
            P(col, row),
            P(row, col),
            P(),
            P(),
        ),
        out_specs=(
            P(("dp",) + row, col),
            P(col + ("dp",), row),
            P(col + ("dp",), row),
            P(row + ("dp",), col),
        ),
        check_vma=False,
    )
```

```python
import functools
import math
import jax
import jax.numpy as jnp
from jax import lax
from jax.experimental import pallas as pl
from jax.experimental.pallas import tpu as pltpu
from jax.sharding import Mesh, PartitionSpec as P

SEQ = 256
N_Y, N_CORE, N_X, N_Z = 4, 2, 4, 8


def contract_last(left, right):
    return lax.dot_general(
        left, right, (((1,), (1,)), ((), ())), preferred_element_type=jnp.float32
    )


def live_mask(assignment, pair_lengths, row_count):
    seq_count = row_count // SEQ
    seq_index = jnp.arange(seq_count, dtype=jnp.int32)
    slot_table = jnp.arange(assignment.shape[0], dtype=jnp.int32)
    pair_ids = jnp.sum(
        jnp.where(slot_table[None, :] == seq_index[:, None] // 2, assignment[None, :], 0), axis=1
    )
    entry_ids = 2 * pair_ids + seq_index % 2
    entry_table = jnp.arange(pair_lengths.shape[0], dtype=jnp.int32)
    live_len = jnp.sum(
        jnp.where(entry_table[None, :] == entry_ids[:, None], pair_lengths[None, :], 0), axis=1
    )
    position = jnp.arange(SEQ, dtype=jnp.int32)
    return position[None, :] < live_len[:, None]


def shift(value, axis, size, step):
    return lax.ppermute(value, axis, [(i, (i + step) % size) for i in range(size)])


def spread(value, axis, size):
    copies = jnp.broadcast_to(value[None], (size,) + value.shape)
    return lax.all_to_all(copies, axis, split_axis=0, concat_axis=0, tiled=True)


def sum_over(value, axis, size):
    blocks = value.reshape(size, value.shape[0] // size, value.shape[1])
    received = lax.all_to_all(blocks, axis, split_axis=0, concat_axis=0, tiled=True)
    return jnp.sum(received, axis=0, dtype=jnp.float32).astype(jnp.bfloat16)


def gather_x(block):
    x = lax.axis_index("x")
    left, right = shift(block, "x", N_X, 1), shift(block, "x", N_X, -1)
    far = jnp.stack([shift(left[0], "x", N_X, 1), shift(right[1], "x", N_X, -1)])
    out = jnp.zeros((N_X,) + block.shape, block.dtype)
    for step, part in ((0, block), (N_X - 1, left), (1, right), (2, far)):
        out = lax.dynamic_update_slice_in_dim(out, part[None], (x + step) % N_X, 0)
    return out


def swiglu_terms(saved_ref):
    pair = saved_ref[0].astype(jnp.float32)
    rows, ffw = pair.shape[0] * pair.shape[2], pair.shape[3]
    gate, up = pair[:, 0].reshape(rows, ffw), pair[:, 1].reshape(rows, ffw)
    sig = jax.nn.sigmoid(gate)
    silu = gate * sig
    return up, sig, silu, up * sig * (1.0 + gate * (1.0 - sig))


def input_kernel(head_ref, saved_ref, w_gate_ref, w_up_ref, out_ref):
    head = head_ref[0].astype(jnp.float32)
    _, _, silu, slope = swiglu_terms(saved_ref)
    grad_gate, grad_up = (head * slope).astype(jnp.bfloat16), (head * silu).astype(jnp.bfloat16)
    term = jnp.dot(grad_gate, w_gate_ref[...], preferred_element_type=jnp.float32)
    term += jnp.dot(grad_up, w_up_ref[...], preferred_element_type=jnp.float32)
    out_ref[...] = term.astype(jnp.bfloat16)


def input_term(head, saved, w_gate, w_up):
    chunks, rows, ffw = head.shape
    width = w_gate.shape[1]
    whole = pl.BlockSpec((ffw, width), lambda i: (0, 0))
    return pl.pallas_call(
        input_kernel,
        grid=(chunks,),
        in_specs=[
            pl.BlockSpec((1, rows, ffw), lambda i: (i, 0, 0)),
            pl.BlockSpec((1,) + saved.shape[1:], lambda i: (i, 0, 0, 0, 0)),
            whole,
            whole,
        ],
        out_specs=pl.BlockSpec((rows, width), lambda i: (i, 0)),
        out_shape=jax.ShapeDtypeStruct((chunks * rows, width), jnp.bfloat16),
        name="input_term",
        cost_estimate=pl.CostEstimate(
            flops=4 * chunks * rows * ffw * width,
            bytes_accessed=2 * (3 * head.size + 2 * w_gate.size + chunks * rows * width),
            transcendentals=head.size,
        ),
    )(head, saved, w_gate, w_up)


def weight_kernel(
    scale, head_own, head_away, saved_own, saved_away, act_own, act_away, cot_own, cot_away,
    gate_ref, up_ref, down_ref, gate_acc, up_acc, down_acc,
):
    @pl.when(pl.program_id(0) == 0)
    def _():
        gate_acc[...] = jnp.zeros_like(gate_acc)
        up_acc[...] = jnp.zeros_like(up_acc)
        down_acc[...] = jnp.zeros_like(down_acc)

    for head_ref, saved_ref, act_ref, cot_ref in (
        (head_own, saved_own, act_own, cot_own),
        (head_away, saved_away, act_away, cot_away),
    ):
        head = head_ref[0].astype(jnp.float32)
        up, _, silu, slope = swiglu_terms(saved_ref)
        hidden = (silu * up).astype(jnp.bfloat16)
        grad_gate = (head * slope).astype(jnp.bfloat16)
        grad_up = (head * silu).astype(jnp.bfloat16)
        act, cot = act_ref[...], cot_ref[...]
        gate_acc[...] += jnp.dot(act, grad_gate, preferred_element_type=jnp.float32)
        up_acc[...] += jnp.dot(act, grad_up, preferred_element_type=jnp.float32)
        down_acc[...] += jnp.dot(cot, hidden, preferred_element_type=jnp.float32)

    @pl.when(pl.program_id(0) == pl.num_programs(0) - 1)
    def _():
        gate_ref[...] = (gate_acc[...] * scale).T.astype(jnp.bfloat16)
        up_ref[...] = (up_acc[...] * scale).T.astype(jnp.bfloat16)
        down_ref[...] = (down_acc[...] * scale).T.astype(jnp.bfloat16)


def weight_grads(scale, head_own, head_away, saved_own, saved_away, acts, cots):
    chunks, rows, ffw = head_own.shape
    half, width = acts[0].shape[0], cots[0].shape[0]
    head_spec = pl.BlockSpec((1, rows, ffw), lambda i: (i, 0, 0))
    saved_spec = pl.BlockSpec((1,) + saved_own.shape[1:], lambda i: (i, 0, 0, 0, 0))
    act_spec = pl.BlockSpec((half, rows), lambda i: (0, i))
    cot_spec = pl.BlockSpec((width, rows), lambda i: (0, i))
    out = lambda cols: pl.BlockSpec((ffw, cols), lambda i: (0, 0))
    shape = lambda cols: jax.ShapeDtypeStruct((ffw, cols), jnp.bfloat16)
    return pl.pallas_call(
        functools.partial(weight_kernel, scale),
        grid=(chunks,),
        in_specs=[head_spec] * 2 + [saved_spec] * 2 + [act_spec] * 2 + [cot_spec] * 2,
        out_specs=[out(half), out(half), out(width)],
        out_shape=[shape(half), shape(half), shape(width)],
        scratch_shapes=[
            pltpu.VMEM((half, ffw), jnp.float32),
            pltpu.VMEM((half, ffw), jnp.float32),
            pltpu.VMEM((width, ffw), jnp.float32),
        ],
        name="weight_grads",
        cost_estimate=pl.CostEstimate(
            flops=4 * chunks * rows * ffw * (2 * half + width),
            bytes_accessed=2 * (6 * head_own.size + 2 * acts[0].size + 2 * cots[0].size),
            transcendentals=2 * head_own.size,
        ),
    )(head_own, head_away, saved_own, saved_away, *acts, *cots)


def on_device(
    activations, cotangent, gate_saved, up_saved, w_gate, w_up, w_down, assignment, pair_lengths
):
    batch = lax.axis_index("dp")
    rows, width = cotangent.shape
    half = width // 2
    own, ffw = gate_saved.shape
    row_axes = ("y", "core")
    n_row = N_Y * N_CORE
    tok = rows * n_row
    n_dp = 2
    away = 1 - batch

    def pick(value, index):
        return lax.dynamic_index_in_dim(value, index, 0, keepdims=False)

    act_own = lax.dynamic_slice_in_dim(activations, batch * half, half, 1)
    act_other = lax.dynamic_slice_in_dim(activations, away * half, half, 1)
    partner = shift(jnp.concatenate([cotangent, act_other], axis=1), "dp", n_dp, 1)

    saved = jnp.stack([gate_saved, up_saved])[None]
    saved = lax.all_gather(saved, ("dp", "z"), axis=0, tiled=True)

    live = live_mask(assignment, pair_lengths, n_dp * tok).reshape(n_dp, tok)
    zero = jnp.zeros((), cotangent.dtype)

    cot_own = spread(cotangent, row_axes, n_row).reshape(tok, width)
    masked_own = jnp.where(pick(live, batch)[:, None], cot_own, zero)
    block_term = contract_last(masked_own, w_down).astype(jnp.bfloat16)
    head_x = sum_over(block_term, "x", N_X)
    _, saved, partner = lax.optimization_barrier((head_x, saved, partner))
    saved = saved.reshape(n_dp, N_Z, 2, own, ffw)
    saved_own, saved_away = pick(saved, batch), pick(saved, away)
    saved_own = lax.all_gather(saved_own, "x", axis=0)
    saved_away = lax.all_gather(saved_away, "x", axis=0)

    rest = spread(jnp.concatenate([partner, act_own], axis=1), row_axes, n_row)
    rest = rest.reshape(tok, 2 * width)
    masked_away = jnp.where(pick(live, away)[:, None], rest[:, :width], zero)
    act_away = rest[:, width : width + half]
    act_here = rest[:, width + half :]

    acts = lax.optimization_barrier((act_here.T, act_away.T))
    cots = lax.optimization_barrier((masked_own.T, masked_away.T))

    head = sum_over(head_x, "z", N_Z)
    head = lax.all_gather(head, ("dp", "z"), axis=0, tiled=True)
    head = head.reshape(n_dp, N_Z * own, ffw)
    head_own = spread(pick(head, batch), "x", N_X)
    halves = (2, N_Z * own // 2, ffw)
    head_away = gather_x(pick(head, away).reshape(halves))

    head_away = head_away.reshape(N_X, N_Z * own, ffw)
    term = input_term(head_own, saved_own, w_gate.T, w_up.T)
    input_grad = sum_over(term, row_axes, n_row)

    scale = 1.0 / math.sqrt(n_dp * tok)
    gate_grad, up_grad, down_grad = weight_grads(
        scale, head_own, head_away, saved_own, saved_away, acts, cots
    )
    f_half = ffw // 2
    down_grad = lax.dynamic_slice_in_dim(down_grad, batch * f_half, f_half, 0)
    return input_grad, gate_grad.T, up_grad.T, down_grad


def solution(mesh):
    fine = Mesh(
        mesh.devices.reshape(2, N_Y, N_CORE, N_X, N_Z), ("dp", "y", "core", "x", "z")
    )
    row, col = ("y", "core"), ("x", "z")

    return jax.shard_map(
        on_device,
        mesh=fine,
        in_specs=(
            P(("dp",) + row, col),
            P(("dp",) + row, col),
            P(("dp",) + col, row),
            P(("dp",) + col, row),
            P(col, row),
            P(col, row),
            P(row, col),
            P(),
            P(),
        ),
        out_specs=(
            P(("dp",) + row, col),
            P(col + ("dp",), row),
            P(col + ("dp",), row),
            P(row + ("dp",), col),
        ),
        check_vma=False,
    )
```

```python
import functools
import math
import jax
import jax.numpy as jnp
from jax import lax
from jax.experimental import pallas as pl
from jax.experimental.pallas import tpu as pltpu
from jax.sharding import Mesh, PartitionSpec as P

SEQ = 256
N_Y, N_CORE, N_X, N_Z = 4, 2, 4, 8


def contract_last(left, right):
    return lax.dot_general(
        left, right, (((1,), (1,)), ((), ())), preferred_element_type=jnp.float32
    )


def live_mask(assignment, pair_lengths, row_count):
    seq_count = row_count // SEQ
    seq_index = jnp.arange(seq_count, dtype=jnp.int32)
    slot_table = jnp.arange(assignment.shape[0], dtype=jnp.int32)
    pair_ids = jnp.sum(
        jnp.where(slot_table[None, :] == seq_index[:, None] // 2, assignment[None, :], 0), axis=1
    )
    entry_ids = 2 * pair_ids + seq_index % 2
    entry_table = jnp.arange(pair_lengths.shape[0], dtype=jnp.int32)
    live_len = jnp.sum(
        jnp.where(entry_table[None, :] == entry_ids[:, None], pair_lengths[None, :], 0), axis=1
    )
    position = jnp.arange(SEQ, dtype=jnp.int32)
    return position[None, :] < live_len[:, None]


def shift(value, axis, size, step):
    return lax.ppermute(value, axis, [(i, (i + step) % size) for i in range(size)])


def spread(value, axis, size):
    copies = jnp.broadcast_to(value[None], (size,) + value.shape)
    return lax.all_to_all(copies, axis, split_axis=0, concat_axis=0, tiled=True)


def sum_over(value, axis, size):
    blocks = value.reshape(size, value.shape[0] // size, value.shape[1])
    received = lax.all_to_all(blocks, axis, split_axis=0, concat_axis=0, tiled=True)
    return jnp.sum(received, axis=0, dtype=jnp.float32).astype(jnp.bfloat16)


def gather_x(block):
    x = lax.axis_index("x")
    left, right = shift(block, "x", N_X, 1), shift(block, "x", N_X, -1)
    far = jnp.stack([shift(left[0], "x", N_X, 1), shift(right[1], "x", N_X, -1)])
    out = jnp.zeros((N_X,) + block.shape, block.dtype)
    for step, part in ((0, block), (N_X - 1, left), (1, right), (2, far)):
        out = lax.dynamic_update_slice_in_dim(out, part[None], (x + step) % N_X, 0)
    return out


def swiglu_terms(saved_ref):
    pair = saved_ref[0, 0].astype(jnp.float32)
    rows, ffw = pair.shape[0] * pair.shape[2], pair.shape[3]
    gate, up = pair[:, 0].reshape(rows, ffw), pair[:, 1].reshape(rows, ffw)
    sig = jax.nn.sigmoid(gate)
    silu = gate * sig
    return up, sig, silu, up * sig * (1.0 + gate * (1.0 - sig))


def input_kernel(order_ref, head_ref, saved_ref, w_gate_ref, w_up_ref, out_ref):
    head = head_ref[0].astype(jnp.float32)
    _, _, silu, slope = swiglu_terms(saved_ref)
    grad_gate, grad_up = (head * slope).astype(jnp.bfloat16), (head * silu).astype(jnp.bfloat16)
    term = jnp.dot(grad_gate, w_gate_ref[...], preferred_element_type=jnp.float32)
    term += jnp.dot(grad_up, w_up_ref[...], preferred_element_type=jnp.float32)
    out_ref[...] = term.astype(jnp.bfloat16)


def saved_spec(saved, which):
    return pl.BlockSpec(
        (1, 1) + saved.shape[2:], lambda i, order: (i, order[which], 0, 0, 0, 0)
    )


def input_term(order, head, saved, w_gate, w_up):
    chunks, rows, ffw = head.shape
    width = w_gate.shape[1]
    whole = pl.BlockSpec((ffw, width), lambda i, order: (0, 0))
    return pl.pallas_call(
        input_kernel,
        grid_spec=pltpu.PrefetchScalarGridSpec(
            num_scalar_prefetch=1,
            grid=(chunks,),
            in_specs=[
                pl.BlockSpec((1, rows, ffw), lambda i, order: (i, 0, 0)),
                saved_spec(saved, 0),
                whole,
                whole,
            ],
            out_specs=pl.BlockSpec((rows, width), lambda i, order: (i, 0)),
        ),
        out_shape=jax.ShapeDtypeStruct((chunks * rows, width), jnp.bfloat16),
        name="input_term",
        cost_estimate=pl.CostEstimate(
            flops=4 * chunks * rows * ffw * width,
            bytes_accessed=2 * (3 * head.size + 2 * w_gate.size + chunks * rows * width),
            transcendentals=head.size,
        ),
    )(order, head, saved, w_gate, w_up)


def weight_kernel(
    scale, order_ref, head_own, head_away, saved_own, saved_away, act_own, act_away, cot_own, cot_away,
    gate_ref, up_ref, down_ref, gate_acc, up_acc, down_acc,
):
    @pl.when(pl.program_id(0) == 0)
    def _():
        gate_acc[...] = jnp.zeros_like(gate_acc)
        up_acc[...] = jnp.zeros_like(up_acc)
        down_acc[...] = jnp.zeros_like(down_acc)

    for head_ref, saved_ref, act_ref, cot_ref in (
        (head_own, saved_own, act_own, cot_own),
        (head_away, saved_away, act_away, cot_away),
    ):
        head = head_ref[0].astype(jnp.float32)
        up, _, silu, slope = swiglu_terms(saved_ref)
        hidden = (silu * up).astype(jnp.bfloat16)
        grad_gate = (head * slope).astype(jnp.bfloat16)
        grad_up = (head * silu).astype(jnp.bfloat16)
        act, cot = act_ref[...], cot_ref[...]
        gate_acc[...] += jnp.dot(act, grad_gate, preferred_element_type=jnp.float32)
        up_acc[...] += jnp.dot(act, grad_up, preferred_element_type=jnp.float32)
        down_acc[...] += jnp.dot(cot, hidden, preferred_element_type=jnp.float32)

    @pl.when(pl.program_id(0) == pl.num_programs(0) - 1)
    def _():
        gate_ref[...] = (gate_acc[...] * scale).T.astype(jnp.bfloat16)
        up_ref[...] = (up_acc[...] * scale).T.astype(jnp.bfloat16)
        down_ref[...] = (down_acc[...] * scale).T.astype(jnp.bfloat16)


def weight_grads(scale, order, head_own, head_away, saved, acts, cots):
    chunks, rows, ffw = head_own.shape
    half, width = acts[0].shape[0], cots[0].shape[0]
    head_spec = pl.BlockSpec((1, rows, ffw), lambda i, order: (i, 0, 0))
    act_spec = pl.BlockSpec((half, rows), lambda i, order: (0, i))
    cot_spec = pl.BlockSpec((width, rows), lambda i, order: (0, i))
    out = lambda cols: pl.BlockSpec((ffw, cols), lambda i, order: (0, 0))
    shape = lambda cols: jax.ShapeDtypeStruct((ffw, cols), jnp.bfloat16)
    return pl.pallas_call(
        functools.partial(weight_kernel, scale),
        grid_spec=pltpu.PrefetchScalarGridSpec(
            num_scalar_prefetch=1,
            grid=(chunks,),
            in_specs=[head_spec] * 2
            + [saved_spec(saved, 0), saved_spec(saved, 1)]
            + [act_spec] * 2
            + [cot_spec] * 2,
            out_specs=[out(half), out(half), out(width)],
            scratch_shapes=[
                pltpu.VMEM((half, ffw), jnp.float32),
                pltpu.VMEM((half, ffw), jnp.float32),
                pltpu.VMEM((width, ffw), jnp.float32),
            ],
        ),
        out_shape=[shape(half), shape(half), shape(width)],
        name="weight_grads",
        cost_estimate=pl.CostEstimate(
            flops=4 * chunks * rows * ffw * (2 * half + width),
            bytes_accessed=2 * (6 * head_own.size + 2 * acts[0].size + 2 * cots[0].size),
            transcendentals=2 * head_own.size,
        ),
    )(order, head_own, head_away, saved, saved, *acts, *cots)


def on_device(
    activations, cotangent, gate_saved, up_saved, w_gate, w_up, w_down, assignment, pair_lengths
):
    batch = lax.axis_index("dp")
    rows, width = cotangent.shape
    half = width // 2
    own, ffw = gate_saved.shape
    row_axes = ("y", "core")
    n_row = N_Y * N_CORE
    tok = rows * n_row
    n_dp = 2
    away = 1 - batch
    order = jnp.stack([batch, away]).astype(jnp.int32)

    def pick(value, index):
        return lax.dynamic_index_in_dim(value, index, 0, keepdims=False)

    act_own = lax.dynamic_slice_in_dim(activations, batch * half, half, 1)
    act_other = lax.dynamic_slice_in_dim(activations, away * half, half, 1)
    partner = shift(jnp.concatenate([cotangent, act_other], axis=1), "dp", n_dp, 1)

    saved = jnp.stack([gate_saved, up_saved])[None]
    saved = lax.all_gather(saved, ("x", "dp", "z"), axis=0, tiled=True)
    saved = saved.reshape(N_X, n_dp, N_Z, 2, own, ffw)

    live = live_mask(assignment, pair_lengths, n_dp * tok).reshape(n_dp, tok)
    zero = jnp.zeros((), cotangent.dtype)

    cot_own = spread(cotangent, row_axes, n_row).reshape(tok, width)
    masked_own = jnp.where(pick(live, batch)[:, None], cot_own, zero)
    block_term = contract_last(masked_own, w_down).astype(jnp.bfloat16)
    head_x = sum_over(block_term, "x", N_X)
    _, partner = lax.optimization_barrier((head_x, partner))

    rest = spread(jnp.concatenate([partner, act_own], axis=1), row_axes, n_row)
    rest = rest.reshape(tok, 2 * width)
    masked_away = jnp.where(pick(live, away)[:, None], rest[:, :width], zero)
    act_away = rest[:, width : width + half]
    act_here = rest[:, width + half :]

    acts = lax.optimization_barrier((act_here.T, act_away.T))
    cots = lax.optimization_barrier((masked_own.T, masked_away.T))

    head = sum_over(head_x, "z", N_Z)
    head = lax.all_gather(head, ("dp", "z"), axis=0, tiled=True)
    head = head.reshape(n_dp, N_Z * own, ffw)
    head_own = spread(pick(head, batch), "x", N_X)
    halves = (2, N_Z * own // 2, ffw)
    head_away = gather_x(pick(head, away).reshape(halves))

    head_away = head_away.reshape(N_X, N_Z * own, ffw)
    term = input_term(order, head_own, saved, w_gate.T, w_up.T)
    input_grad = sum_over(term, row_axes, n_row)

    scale = 1.0 / math.sqrt(n_dp * tok)
    gate_grad, up_grad, down_grad = weight_grads(
        scale, order, head_own, head_away, saved, acts, cots
    )
    f_half = ffw // 2
    down_grad = lax.dynamic_slice_in_dim(down_grad, batch * f_half, f_half, 0)
    return input_grad, gate_grad.T, up_grad.T, down_grad


def solution(mesh):
    fine = Mesh(
        mesh.devices.reshape(2, N_Y, N_CORE, N_X, N_Z), ("dp", "y", "core", "x", "z")
    )
    row, col = ("y", "core"), ("x", "z")

    return jax.shard_map(
        on_device,
        mesh=fine,
        in_specs=(
            P(("dp",) + row, col),
            P(("dp",) + row, col),
            P(("dp",) + col, row),
            P(("dp",) + col, row),
            P(col, row),
            P(col, row),
            P(row, col),
            P(),
            P(),
        ),
        out_specs=(
            P(("dp",) + row, col),
            P(col + ("dp",), row),
            P(col + ("dp",), row),
            P(row + ("dp",), col),
        ),
        check_vma=False,
    )
```

```python
import functools
import math
import jax
import jax.numpy as jnp
from jax import lax
from jax.experimental import pallas as pl
from jax.experimental.pallas import tpu as pltpu
from jax.sharding import Mesh, PartitionSpec as P

N_Y, N_CORE, N_X, N_Z = 4, 2, 4, 8


def shift(value, axis, size, step):
    return lax.ppermute(value, axis, [(i, (i + step) % size) for i in range(size)])


def spread(value, axis, size):
    copies = jnp.broadcast_to(value[None], (size,) + value.shape)
    return lax.all_to_all(copies, axis, split_axis=0, concat_axis=0, tiled=True)


def sum_over(value, axis, size):
    blocks = value.reshape(size, value.shape[0] // size, value.shape[1])
    received = lax.all_to_all(blocks, axis, split_axis=0, concat_axis=0, tiled=True)
    return jnp.sum(received, axis=0, dtype=jnp.float32).astype(jnp.bfloat16)


def live_length(order_ref, assignment_ref, lengths_ref, which, chunk):
    slot = 2 * order_ref[which] + lax.div(chunk, 2)
    return lengths_ref[2 * assignment_ref[slot] + lax.rem(chunk, 2)]


def rows_below(shape, count):
    return lax.broadcasted_iota(jnp.int32, shape, 0) < count


def head_kernel(order_ref, assignment_ref, lengths_ref, cot_ref, w_ref, out_ref):
    live = live_length(order_ref, assignment_ref, lengths_ref, 0, pl.program_id(0))
    cot = cot_ref[...]
    masked = jnp.where(rows_below(cot.shape, live), cot, jnp.zeros_like(cot))
    term = lax.dot_general(
        masked, w_ref[...], (((1,), (1,)), ((), ())), preferred_element_type=jnp.float32
    )
    ffw = w_ref.shape[0]
    out_ref[0, :, :ffw] = term.astype(jnp.bfloat16)
    out_ref[0, :, ffw:] = jnp.zeros((term.shape[0], out_ref.shape[2] - ffw), jnp.bfloat16)


def head_term(scalars, cot, w_down, lanes):
    tok, width = cot.shape
    ffw = w_down.shape[0]
    rows = tok // N_X
    return pl.pallas_call(
        head_kernel,
        grid_spec=pltpu.PrefetchScalarGridSpec(
            num_scalar_prefetch=3,
            grid=(N_X,),
            in_specs=[
                pl.BlockSpec((rows, width), lambda i, *_: (i, 0)),
                pl.BlockSpec((ffw, width), lambda i, *_: (0, 0)),
            ],
            out_specs=pl.BlockSpec((1, rows, lanes), lambda i, *_: (i, 0, 0)),
        ),
        out_shape=jax.ShapeDtypeStruct((N_X, rows, lanes), jnp.bfloat16),
        name="head_term",
        cost_estimate=pl.CostEstimate(
            flops=2 * tok * width * ffw,
            bytes_accessed=2 * (cot.size + w_down.size + tok * lanes),
            transcendentals=0,
        ),
    )(*scalars, cot, w_down)


def swiglu_terms(saved_ref):
    pair = saved_ref[0, 0].astype(jnp.float32)
    rows, ffw = pair.shape[0] * pair.shape[2], pair.shape[3]
    gate, up = pair[:, 0].reshape(rows, ffw), pair[:, 1].reshape(rows, ffw)
    sig = jax.nn.sigmoid(gate)
    silu = gate * sig
    return up, silu, up * sig * (1.0 + gate * (1.0 - sig))


def input_kernel(order_ref, head_ref, saved_ref, w_gate_ref, w_up_ref, out_ref):
    ffw = w_gate_ref.shape[0]
    head = head_ref[0, :, :ffw].astype(jnp.float32)
    _, silu, slope = swiglu_terms(saved_ref)
    grad_gate, grad_up = (head * slope).astype(jnp.bfloat16), (head * silu).astype(jnp.bfloat16)
    term = jnp.dot(grad_gate, w_gate_ref[...], preferred_element_type=jnp.float32)
    term += jnp.dot(grad_up, w_up_ref[...], preferred_element_type=jnp.float32)
    out_ref[...] = term.astype(jnp.bfloat16)


def input_term(order, head, saved, w_gate, w_up):
    chunks, rows, lanes = head.shape
    ffw, width = w_gate.shape
    whole = pl.BlockSpec((ffw, width), lambda i, order: (0, 0))
    return pl.pallas_call(
        input_kernel,
        grid_spec=pltpu.PrefetchScalarGridSpec(
            num_scalar_prefetch=1,
            grid=(chunks,),
            in_specs=[
                pl.BlockSpec((1, rows, lanes), lambda i, order: (i, 0, 0)),
                pl.BlockSpec(
                    (1, 1) + saved.shape[2:], lambda i, order: (i, order[0], 0, 0, 0, 0)
                ),
                whole,
                whole,
            ],
            out_specs=pl.BlockSpec((rows, width), lambda i, order: (i, 0)),
        ),
        out_shape=jax.ShapeDtypeStruct((chunks * rows, width), jnp.bfloat16),
        name="input_term",
        cost_estimate=pl.CostEstimate(
            flops=4 * chunks * rows * ffw * width,
            bytes_accessed=2 * (3 * head.size + 2 * w_gate.size + chunks * rows * width),
            transcendentals=head.size,
        ),
    )(order, head, saved, w_gate, w_up)


def weight_kernel(
    scale, order_ref, assignment_ref, lengths_ref,
    head_own, here, left, right, far_low, far_high,
    saved_own, saved_away, act_own, act_away, cot_own, cot_away,
    gate_ref, up_ref, down_ref, gate_acc, up_acc, down_acc, head_away,
):
    step = pl.program_id(0)
    chunk = order_ref[2 + step]
    mid = far_low.shape[0]

    @pl.when(step == 0)
    def _():
        gate_acc[...] = jnp.zeros_like(gate_acc)
        up_acc[...] = jnp.zeros_like(up_acc)
        down_acc[...] = jnp.zeros_like(down_acc)

    for index, part in enumerate((here, left, right)):
        @pl.when(step == index)
        def _(part=part):
            head_away[:mid, :] = part[0]
            head_away[mid:, :] = part[1]

    @pl.when(step == 3)
    def _():
        head_away[:mid, :] = far_low[...]
        head_away[mid:, :] = far_high[...]

    def contract(left_rows, right_rows):
        return lax.dot_general(
            left_rows, right_rows, (((0,), (0,)), ((), ())), preferred_element_type=jnp.float32
        )

    ffw = gate_acc.shape[1]
    for which, head_rows, saved_ref, act_ref, cot_ref in (
        (0, head_own[0], saved_own, act_own, cot_own),
        (1, head_away[...], saved_away, act_away, cot_away),
    ):
        head = head_rows[:, :ffw].astype(jnp.float32)
        up, silu, slope = swiglu_terms(saved_ref)
        live = live_length(order_ref, assignment_ref, lengths_ref, which, chunk)
        cot = cot_ref[...]
        masked = jnp.where(rows_below(cot.shape, live), cot, jnp.zeros_like(cot))
        act = act_ref[...]
        gate_acc[...] += contract(act, (head * slope).astype(jnp.bfloat16))
        up_acc[...] += contract(act, (head * silu).astype(jnp.bfloat16))
        down_acc[...] += contract((silu * up).astype(jnp.bfloat16), masked)

    @pl.when(step == pl.num_programs(0) - 1)
    def _():
        gate_ref[...] = (gate_acc[...] * scale).T.astype(jnp.bfloat16)
        up_ref[...] = (up_acc[...] * scale).T.astype(jnp.bfloat16)
        f_half = down_ref.shape[0]
        first = pl.multiple_of(order_ref[0] * f_half, f_half)
        down_ref[...] = (down_acc[pl.ds(first, f_half), :] * scale).astype(jnp.bfloat16)


def weight_grads(scale, scalars, head_own, head_away, saved, cot, rest):
    chunks, rows, lanes = head_own.shape
    ffw, width = saved.shape[-1], cot.shape[1]
    half = width // 2
    whole = lambda value: pl.BlockSpec(value.shape, lambda i, *_: (0,) * value.ndim)
    saved_spec = lambda which: pl.BlockSpec(
        (1, 1) + saved.shape[2:],
        lambda i, order, *_: (order[2 + i], order[which], 0, 0, 0, 0),
    )
    column = lambda cols, index: pl.BlockSpec(
        (rows, cols), lambda i, order, *_: (order[2 + i], index)
    )
    out = lambda *shape: pl.BlockSpec(shape, lambda i, *_: (0, 0))
    shape = lambda *dims: jax.ShapeDtypeStruct(dims, jnp.bfloat16)
    return pl.pallas_call(
        functools.partial(weight_kernel, scale),
        grid_spec=pltpu.PrefetchScalarGridSpec(
            num_scalar_prefetch=3,
            grid=(chunks,),
            in_specs=[pl.BlockSpec((1, rows, lanes), lambda i, order, *_: (order[2 + i], 0, 0))]
            + [whole(part) for part in head_away]
            + [saved_spec(0), saved_spec(1)]
            + [column(half, 3), column(half, 2), column(width, 0), column(width, 0)],
            out_specs=[out(ffw, half), out(ffw, half), out(ffw // 2, width)],
            scratch_shapes=[
                pltpu.VMEM((half, ffw), jnp.float32),
                pltpu.VMEM((half, ffw), jnp.float32),
                pltpu.VMEM((ffw, width), jnp.float32),
                pltpu.VMEM((rows, lanes), jnp.bfloat16),
            ],
        ),
        out_shape=[shape(ffw, half), shape(ffw, half), shape(ffw // 2, width)],
        name="weight_grads",
        cost_estimate=pl.CostEstimate(
            flops=4 * chunks * rows * ffw * 2 * width,
            bytes_accessed=2 * (6 * head_own.size + cot.size + rest.size),
            transcendentals=2 * head_own.size,
        ),
    )(*scalars, head_own, *head_away, saved, saved, rest, rest, cot, rest)


def on_device(
    activations, cotangent, gate_saved, up_saved, w_gate, w_up, w_down, assignment, pair_lengths
):
    batch, x = lax.axis_index("dp"), lax.axis_index("x")
    away = 1 - batch
    rows, width = cotangent.shape
    half = width // 2
    own, ffw = gate_saved.shape
    lanes = -(-ffw // 128) * 128
    row_axes = ("y", "core")
    n_row = N_Y * N_CORE
    tok = rows * n_row
    n_dp = 2
    order = jnp.stack([batch, away] + [(x + step) % N_X for step in (0, N_X - 1, 1, 2)])
    order = order.astype(jnp.int32)
    scalars = (order, assignment, pair_lengths)

    def pick(value, index):
        return lax.dynamic_index_in_dim(value, index, 0, keepdims=False)

    act_own = lax.dynamic_slice_in_dim(activations, batch * half, half, 1)
    act_other = lax.dynamic_slice_in_dim(activations, away * half, half, 1)
    partner = shift(jnp.concatenate([cotangent, act_other], axis=1), "dp", n_dp, 1)

    saved = jnp.stack([gate_saved, up_saved])[None]
    saved = lax.all_gather(saved, ("x", "dp", "z"), axis=0, tiled=True)
    saved = saved.reshape(N_X, n_dp, N_Z, 2, own, ffw)

    cot_own = spread(cotangent, row_axes, n_row).reshape(tok, width)
    block_term = head_term(scalars, cot_own, w_down, lanes)
    head_x = sum_over(block_term.reshape(tok, lanes), "x", N_X)
    _, partner = lax.optimization_barrier((head_x, partner))
    rest = spread(jnp.concatenate([partner, act_own], axis=1), row_axes, n_row)
    rest = rest.reshape(tok, 2 * width)

    head = sum_over(head_x, "z", N_Z)
    head = lax.all_gather(head, ("dp", "z"), axis=0, tiled=True)
    head = head.reshape(n_dp, N_Z * own, lanes)
    head_own = spread(pick(head, batch), "x", N_X)
    here = pick(head, away).reshape(2, N_Z * own // 2, lanes)
    left, right = shift(here, "x", N_X, 1), shift(here, "x", N_X, -1)
    far_low, far_high = shift(left[0], "x", N_X, 1), shift(right[1], "x", N_X, -1)
    head_away = (here, left, right, far_low, far_high)

    term = input_term(order, head_own, saved, w_gate.T, w_up.T)
    input_grad = sum_over(term, row_axes, n_row)

    scale = 1.0 / math.sqrt(n_dp * tok)
    gate_grad, up_grad, down_grad = weight_grads(
        scale, scalars, head_own, head_away, saved, cot_own, rest
    )
    return input_grad, gate_grad.T, up_grad.T, down_grad


def solution(mesh):
    fine = Mesh(
        mesh.devices.reshape(2, N_Y, N_CORE, N_X, N_Z), ("dp", "y", "core", "x", "z")
    )
    row, col = ("y", "core"), ("x", "z")

    return jax.shard_map(
        on_device,
        mesh=fine,
        in_specs=(
            P(("dp",) + row, col),
            P(("dp",) + row, col),
            P(("dp",) + col, row),
            P(("dp",) + col, row),
            P(col, row),
            P(col, row),
            P(row, col),
            P(),
            P(),
        ),
        out_specs=(
            P(("dp",) + row, col),
            P(col + ("dp",), row),
            P(col + ("dp",), row),
            P(row + ("dp",), col),
        ),
        check_vma=False,
    )
```

```python
import functools
import math
import jax
import jax.numpy as jnp
from jax import lax
from jax.experimental import pallas as pl
from jax.experimental.pallas import tpu as pltpu
from jax.sharding import Mesh, PartitionSpec as P

N_Y, N_CORE, N_X, N_Z = 4, 2, 4, 8


def shift(value, axis, size, step):
    return lax.ppermute(value, axis, [(i, (i + step) % size) for i in range(size)])


def spread(value, axis, size):
    copies = jnp.broadcast_to(value[None], (size,) + value.shape)
    return lax.all_to_all(copies, axis, split_axis=0, concat_axis=0, tiled=True)


def sum_over(value, axis, size):
    blocks = value.reshape(size, value.shape[0] // size, value.shape[1])
    received = lax.all_to_all(blocks, axis, split_axis=0, concat_axis=0, tiled=True)
    return jnp.sum(received, axis=0, dtype=jnp.float32).astype(jnp.bfloat16)


def live_length(order_ref, assignment_ref, lengths_ref, which, chunk):
    slot = 2 * order_ref[which] + lax.div(chunk, 2)
    return lengths_ref[2 * assignment_ref[slot] + lax.rem(chunk, 2)]


def rows_below(shape, count):
    return lax.broadcasted_iota(jnp.int32, shape, 0) < count


def head_kernel(order_ref, assignment_ref, lengths_ref, cot_ref, w_ref, out_ref):
    ffw = w_ref.shape[0]
    chunks, rows, lanes = out_ref.shape
    w_turned = w_ref[...].T
    for chunk in range(chunks):
        live = live_length(order_ref, assignment_ref, lengths_ref, 0, jnp.int32(chunk))
        cot = cot_ref[chunk * rows : (chunk + 1) * rows, :]
        masked = jnp.where(rows_below(cot.shape, live), cot, jnp.zeros_like(cot))
        term = jnp.dot(masked, w_turned, preferred_element_type=jnp.float32)
        out_ref[chunk, :, :ffw] = term.astype(jnp.bfloat16)
        out_ref[chunk, :, ffw:] = jnp.zeros((rows, lanes - ffw), jnp.bfloat16)


def head_term(scalars, cot, w_down, lanes):
    tok, width = cot.shape
    ffw = w_down.shape[0]
    return pl.pallas_call(
        head_kernel,
        in_specs=[pl.BlockSpec(memory_space=pltpu.SMEM)] * 3
        + [pl.BlockSpec(memory_space=pltpu.VMEM)] * 2,
        out_specs=pl.BlockSpec(memory_space=pltpu.VMEM),
        out_shape=jax.ShapeDtypeStruct((N_X, tok // N_X, lanes), jnp.bfloat16),
        name="head_term",
        cost_estimate=pl.CostEstimate(
            flops=2 * tok * width * ffw,
            bytes_accessed=2 * (cot.size + w_down.size + tok * lanes),
            transcendentals=0,
        ),
    )(*scalars, cot, w_down)


def take_part(step, parts, head_ref):
    here, left, right, far_low, far_high = parts
    mid = far_low.shape[0]
    for index, part in enumerate((here, left, right)):
        @pl.when(step == index)
        def _(part=part):
            head_ref[:mid, :] = part[0]
            head_ref[mid:, :] = part[1]

    @pl.when(step == 3)
    def _():
        head_ref[:mid, :] = far_low[...]
        head_ref[mid:, :] = far_high[...]


def whole(value):
    return pl.BlockSpec(value.shape, lambda i, *_: (0,) * value.ndim)


def saved_block(saved, which):
    return pl.BlockSpec(
        (1, 1) + saved.shape[2:], lambda i, order, *_: (order[2 + i], order[which], 0, 0, 0, 0)
    )


def swiglu_terms(saved_ref):
    pair = saved_ref[0, 0].astype(jnp.float32)
    rows, ffw = pair.shape[0] * pair.shape[2], pair.shape[3]
    gate, up = pair[:, 0].reshape(rows, ffw), pair[:, 1].reshape(rows, ffw)
    sig = jax.nn.sigmoid(gate)
    silu = gate * sig
    return up, silu, up * sig * (1.0 + gate * (1.0 - sig))


def gradients(head_ref, saved_ref):
    up, silu, slope = swiglu_terms(saved_ref)
    head = head_ref[:, : up.shape[1]].astype(jnp.float32)
    return (
        (head * slope).astype(jnp.bfloat16),
        (head * silu).astype(jnp.bfloat16),
        (silu * up).astype(jnp.bfloat16),
    )


def input_kernel(
    order_ref, here, left, right, far_low, far_high, saved_ref, w_gate_ref, w_up_ref,
    out_ref, gate_ref, up_ref, hidden_ref, head_ref,
):
    take_part(pl.program_id(0), (here, left, right, far_low, far_high), head_ref)
    grad_gate, grad_up, hidden = gradients(head_ref, saved_ref)
    term = jnp.dot(grad_gate, w_gate_ref[...], preferred_element_type=jnp.float32)
    term += jnp.dot(grad_up, w_up_ref[...], preferred_element_type=jnp.float32)
    out_ref[...] = term.astype(jnp.bfloat16)
    gate_ref[...] = grad_gate
    up_ref[...] = grad_up
    hidden_ref[...] = hidden


def input_term(order, head, saved, w_gate, w_up):
    rows, lanes = 2 * head[0].shape[1], head[0].shape[2]
    ffw, width = w_gate.shape
    tok = N_X * rows
    kept = pl.BlockSpec((rows, ffw), lambda i, order: (i, 0))
    return pl.pallas_call(
        input_kernel,
        grid_spec=pltpu.PrefetchScalarGridSpec(
            num_scalar_prefetch=1,
            grid=(N_X,),
            in_specs=[whole(part) for part in head]
            + [saved_block(saved, 0), whole(w_gate), whole(w_up)],
            out_specs=[
                pl.BlockSpec((rows, width), lambda i, order: (order[2 + i], 0)), kept, kept, kept
            ],
            scratch_shapes=[pltpu.VMEM((rows, lanes), jnp.bfloat16)],
        ),
        out_shape=[jax.ShapeDtypeStruct((tok, width), jnp.bfloat16)]
        + [jax.ShapeDtypeStruct((tok, ffw), jnp.bfloat16)] * 3,
        name="input_term",
        cost_estimate=pl.CostEstimate(
            flops=4 * tok * ffw * width,
            bytes_accessed=2 * (6 * tok * ffw + 2 * w_gate.size + tok * width),
            transcendentals=tok * ffw,
        ),
    )(order, *head, saved, w_gate, w_up)


def weight_kernel(
    scale, order_ref, assignment_ref, lengths_ref,
    gate_own, up_own, hidden_own, here, left, right, far_low, far_high, saved_away,
    act_own, act_away, cot_own, cot_away,
    gate_ref, up_ref, down_ref, gate_acc, up_acc, down_acc, head_ref,
):
    step = pl.program_id(0)
    chunk = order_ref[2 + step]

    @pl.when(step == 0)
    def _():
        gate_acc[...] = jnp.zeros_like(gate_acc)
        up_acc[...] = jnp.zeros_like(up_acc)
        down_acc[...] = jnp.zeros_like(down_acc)

    def contract(left_rows, right_rows):
        return lax.dot_general(
            left_rows, right_rows, (((0,), (0,)), ((), ())), preferred_element_type=jnp.float32
        )

    take_part(step, (here, left, right, far_low, far_high), head_ref)
    for which, rows_of, act_ref, cot_ref in (
        (0, lambda: (gate_own[...], up_own[...], hidden_own[...]), act_own, cot_own),
        (1, lambda: gradients(head_ref, saved_away), act_away, cot_away),
    ):
        grad_gate, grad_up, hidden = rows_of()
        live = live_length(order_ref, assignment_ref, lengths_ref, which, chunk)
        cot = cot_ref[...]
        masked = jnp.where(rows_below(cot.shape, live), cot, jnp.zeros_like(cot))
        act = act_ref[...]
        gate_acc[...] += contract(act, grad_gate)
        up_acc[...] += contract(act, grad_up)
        down_acc[...] += contract(hidden, masked)

    @pl.when(step == pl.num_programs(0) - 1)
    def _():
        gate_ref[...] = (gate_acc[...] * scale).T.astype(jnp.bfloat16)
        up_ref[...] = (up_acc[...] * scale).T.astype(jnp.bfloat16)
        f_half = down_ref.shape[0]
        first = pl.multiple_of(order_ref[0] * f_half, f_half)
        down_ref[...] = (down_acc[pl.ds(first, f_half), :] * scale).astype(jnp.bfloat16)


def weight_grads(scale, scalars, own_rows, head_away, saved, cot, rest):
    rows, lanes = 2 * head_away[0].shape[1], head_away[0].shape[2]
    tok, width = cot.shape
    ffw, half = saved.shape[-1], width // 2
    kept = pl.BlockSpec((rows, ffw), lambda i, *_: (i, 0))
    column = lambda cols, index: pl.BlockSpec(
        (rows, cols), lambda i, order, *_: (order[2 + i], index)
    )
    out = lambda *shape: pl.BlockSpec(shape, lambda i, *_: (0, 0))
    shape = lambda *dims: jax.ShapeDtypeStruct(dims, jnp.bfloat16)
    return pl.pallas_call(
        functools.partial(weight_kernel, scale),
        grid_spec=pltpu.PrefetchScalarGridSpec(
            num_scalar_prefetch=3,
            grid=(N_X,),
            in_specs=[kept] * 3
            + [whole(part) for part in head_away]
            + [saved_block(saved, 1)]
            + [column(half, 3), column(half, 2), column(width, 0), column(width, 0)],
            out_specs=[out(ffw, half), out(ffw, half), out(ffw // 2, width)],
            scratch_shapes=[
                pltpu.VMEM((half, ffw), jnp.float32),
                pltpu.VMEM((half, ffw), jnp.float32),
                pltpu.VMEM((ffw, width), jnp.float32),
                pltpu.VMEM((rows, lanes), jnp.bfloat16),
            ],
        ),
        out_shape=[shape(ffw, half), shape(ffw, half), shape(ffw // 2, width)],
        name="weight_grads",
        cost_estimate=pl.CostEstimate(
            flops=8 * tok * ffw * width,
            bytes_accessed=2 * (6 * tok * ffw + cot.size + rest.size),
            transcendentals=tok * ffw,
        ),
    )(*scalars, *own_rows, *head_away, saved, rest, rest, cot, rest)


def gather_x(block):
    left, right = shift(block, "x", N_X, 1), shift(block, "x", N_X, -1)
    far_low, far_high = shift(left[0], "x", N_X, 1), shift(right[1], "x", N_X, -1)
    return block, left, right, far_low, far_high


def on_device(
    activations, cotangent, gate_saved, up_saved, w_gate, w_up, w_down, assignment, pair_lengths
):
    batch, x = lax.axis_index("dp"), lax.axis_index("x")
    away = 1 - batch
    rows, width = cotangent.shape
    half = width // 2
    own, ffw = gate_saved.shape
    lanes = -(-ffw // 128) * 128
    row_axes = ("y", "core")
    n_row = N_Y * N_CORE
    tok = rows * n_row
    n_dp = 2
    order = jnp.stack([batch, away] + [(x + step) % N_X for step in (0, N_X - 1, 1, 2)])
    order = order.astype(jnp.int32)
    scalars = (order, assignment, pair_lengths)

    def pick(value, index):
        return lax.dynamic_index_in_dim(value, index, 0, keepdims=False)

    act_own = lax.dynamic_slice_in_dim(activations, batch * half, half, 1)
    act_other = lax.dynamic_slice_in_dim(activations, away * half, half, 1)
    partner = shift(jnp.concatenate([cotangent, act_other], axis=1), "dp", n_dp, 1)

    saved = jnp.stack([gate_saved, up_saved])[None]
    saved = lax.all_gather(saved, ("x", "dp", "z"), axis=0, tiled=True)
    saved = saved.reshape(N_X, n_dp, N_Z, 2, own, ffw)

    cot_own = spread(cotangent, row_axes, n_row).reshape(tok, width)
    block_term = head_term(scalars, cot_own, w_down, lanes)
    head_x = sum_over(block_term.reshape(tok, lanes), "x", N_X)
    _, partner = lax.optimization_barrier((head_x, partner))
    rest = spread(jnp.concatenate([partner, act_own], axis=1), row_axes, n_row)
    rest = rest.reshape(tok, 2 * width)

    head = sum_over(head_x, "z", N_Z)
    head = lax.all_gather(head, ("dp", "z"), axis=0, tiled=True)
    head = head.reshape(n_dp, N_Z * own, lanes)
    halves = (2, N_Z * own // 2, lanes)
    head_own = gather_x(pick(head, batch).reshape(halves))
    head_away = gather_x(pick(head, away).reshape(halves))

    term, *own_rows = input_term(order, head_own, saved, w_gate.T, w_up.T)
    input_grad = sum_over(term, row_axes, n_row)

    scale = 1.0 / math.sqrt(n_dp * tok)
    gate_grad, up_grad, down_grad = weight_grads(
        scale, scalars, own_rows, head_away, saved, cot_own, rest
    )
    return input_grad, gate_grad.T, up_grad.T, down_grad


def solution(mesh):
    fine = Mesh(
        mesh.devices.reshape(2, N_Y, N_CORE, N_X, N_Z), ("dp", "y", "core", "x", "z")
    )
    row, col = ("y", "core"), ("x", "z")

    return jax.shard_map(
        on_device,
        mesh=fine,
        in_specs=(
            P(("dp",) + row, col),
            P(("dp",) + row, col),
            P(("dp",) + col, row),
            P(("dp",) + col, row),
            P(col, row),
            P(col, row),
            P(row, col),
            P(),
            P(),
        ),
        out_specs=(
            P(("dp",) + row, col),
            P(col + ("dp",), row),
            P(col + ("dp",), row),
            P(row + ("dp",), col),
        ),
        check_vma=False,
    )
```

```python
import functools
import math
import jax
import jax.numpy as jnp
from jax import lax
from jax.experimental import pallas as pl
from jax.experimental.pallas import tpu as pltpu
from jax.sharding import Mesh, PartitionSpec as P

N_Y, N_CORE, N_X, N_Z = 4, 2, 4, 8


def shift(value, axis, size, step):
    return lax.ppermute(value, axis, [(i, (i + step) % size) for i in range(size)])


def spread(value, axis, size):
    copies = jnp.broadcast_to(value[None], (size,) + value.shape)
    return lax.all_to_all(copies, axis, split_axis=0, concat_axis=0, tiled=True)


def sum_over(value, axis, size):
    blocks = value.reshape(size, value.shape[0] // size, value.shape[1])
    received = lax.all_to_all(blocks, axis, split_axis=0, concat_axis=0, tiled=True)
    return jnp.sum(received, axis=0, dtype=jnp.float32).astype(jnp.bfloat16)


def live_length(order_ref, assignment_ref, lengths_ref, which, chunk):
    slot = 2 * order_ref[which] + lax.div(chunk, 2)
    return lengths_ref[2 * assignment_ref[slot] + lax.rem(chunk, 2)]


def rows_below(shape, count):
    return lax.broadcasted_iota(jnp.int32, shape, 0) < count


def head_kernel(order_ref, assignment_ref, lengths_ref, cot_ref, w_ref, out_ref):
    ffw = w_ref.shape[0]
    chunks, rows, lanes = out_ref.shape
    w_turned = w_ref[...].T
    for chunk in range(chunks):
        live = live_length(order_ref, assignment_ref, lengths_ref, 0, jnp.int32(chunk))
        cot = cot_ref[chunk * rows : (chunk + 1) * rows, :]
        masked = jnp.where(rows_below(cot.shape, live), cot, jnp.zeros_like(cot))
        term = jnp.dot(masked, w_turned, preferred_element_type=jnp.float32)
        out_ref[chunk, :, :ffw] = term.astype(jnp.bfloat16)
        out_ref[chunk, :, ffw:] = jnp.zeros((rows, lanes - ffw), jnp.bfloat16)


def head_term(scalars, cot, w_down, lanes):
    tok, width = cot.shape
    ffw = w_down.shape[0]
    return pl.pallas_call(
        head_kernel,
        in_specs=[pl.BlockSpec(memory_space=pltpu.SMEM)] * 3
        + [pl.BlockSpec(memory_space=pltpu.VMEM)] * 2,
        out_specs=pl.BlockSpec(memory_space=pltpu.VMEM),
        out_shape=jax.ShapeDtypeStruct((N_X, tok // N_X, lanes), jnp.bfloat16),
        name="head_term",
        cost_estimate=pl.CostEstimate(
            flops=2 * tok * width * ffw,
            bytes_accessed=2 * (cot.size + w_down.size + tok * lanes),
            transcendentals=0,
        ),
    )(*scalars, cot, w_down)


def take_part(step, parts, head_ref):
    here, left, right, far_low, far_high = parts
    mid = far_low.shape[0]
    for index, part in enumerate((here, left, right)):
        @pl.when(step == index)
        def _(part=part):
            head_ref[:mid, :] = part[0]
            head_ref[mid:, :] = part[1]

    @pl.when(step == 3)
    def _():
        head_ref[:mid, :] = far_low[...]
        head_ref[mid:, :] = far_high[...]


def whole(value):
    return pl.BlockSpec(value.shape, lambda i, *_: (0,) * value.ndim)


def saved_block(saved, which):
    return pl.BlockSpec(
        (1, 1) + saved.shape[2:], lambda i, order, *_: (order[2 + i], order[which], 0, 0, 0)
    )


def pack_pair(gate, up):
    body = gate.shape[1] // 128 * 128
    return jnp.concatenate([gate[:, :body], up[:, :body], gate[:, body:], up[:, body:]], axis=1)


def swiglu_terms(saved_ref):
    pair = saved_ref[0, 0]
    pair = pair.reshape(pair.shape[0] * pair.shape[1], pair.shape[2]).astype(jnp.float32)
    ffw = pair.shape[1] // 2
    body = ffw // 128 * 128
    tail = pair[:, 2 * body :]
    turned = pltpu.roll(tail, ffw - body, 1)
    gate = jnp.concatenate([pair[:, :body], tail[:, : ffw - body]], axis=1)
    up = jnp.concatenate([pair[:, body : 2 * body], turned[:, : ffw - body]], axis=1)
    sig = jax.nn.sigmoid(gate)
    silu = gate * sig
    return up, silu, up * sig * (1.0 + gate * (1.0 - sig))


def gradients(head_ref, saved_ref):
    up, silu, slope = swiglu_terms(saved_ref)
    head = head_ref[:, : up.shape[1]].astype(jnp.float32)
    return (
        (head * slope).astype(jnp.bfloat16),
        (head * silu).astype(jnp.bfloat16),
        (silu * up).astype(jnp.bfloat16),
    )


def input_kernel(
    order_ref, here, left, right, far_low, far_high, saved_ref, w_gate_ref, w_up_ref,
    out_ref, head_ref,
):
    take_part(pl.program_id(0), (here, left, right, far_low, far_high), head_ref)
    grad_gate, grad_up, _ = gradients(head_ref, saved_ref)
    term = jnp.dot(grad_gate, w_gate_ref[...], preferred_element_type=jnp.float32)
    term += jnp.dot(grad_up, w_up_ref[...], preferred_element_type=jnp.float32)
    out_ref[...] = term.astype(jnp.bfloat16)


def input_term(order, head, saved, w_gate, w_up):
    rows, lanes = 2 * head[0].shape[1], head[0].shape[2]
    ffw, width = w_gate.shape
    tok = N_X * rows
    return pl.pallas_call(
        input_kernel,
        grid_spec=pltpu.PrefetchScalarGridSpec(
            num_scalar_prefetch=1,
            grid=(N_X,),
            in_specs=[whole(part) for part in head]
            + [saved_block(saved, 0), whole(w_gate), whole(w_up)],
            out_specs=pl.BlockSpec((rows, width), lambda i, order: (order[2 + i], 0)),
            scratch_shapes=[pltpu.VMEM((rows, lanes), jnp.bfloat16)],
        ),
        out_shape=jax.ShapeDtypeStruct((tok, width), jnp.bfloat16),
        name="input_term",
        cost_estimate=pl.CostEstimate(
            flops=4 * tok * ffw * width,
            bytes_accessed=2 * (3 * tok * ffw + 2 * w_gate.size + tok * width),
            transcendentals=tok * ffw,
        ),
    )(order, *head, saved, w_gate, w_up)


def weight_kernel(
    scale, order_ref, assignment_ref, lengths_ref,
    *refs,
):
    parts_own, parts_away, refs = refs[:5], refs[5:10], refs[10:]
    saved_own, saved_away, act_own, act_away, cot_own, cot_away = refs[:6]
    gate_ref, up_ref, down_ref, gate_acc, up_acc, down_acc, head_own, head_away = refs[6:]
    step = pl.program_id(0)
    chunk = order_ref[2 + step]

    @pl.when(step == 0)
    def _():
        gate_acc[...] = jnp.zeros_like(gate_acc)
        up_acc[...] = jnp.zeros_like(up_acc)
        down_acc[...] = jnp.zeros_like(down_acc)

    def contract(left_rows, right_rows):
        return lax.dot_general(
            left_rows, right_rows, (((0,), (0,)), ((), ())), preferred_element_type=jnp.float32
        )

    take_part(step, parts_own, head_own)
    take_part(step, parts_away, head_away)
    for which, head_ref, saved_ref, act_ref, cot_ref in (
        (0, head_own, saved_own, act_own, cot_own),
        (1, head_away, saved_away, act_away, cot_away),
    ):
        grad_gate, grad_up, hidden = gradients(head_ref, saved_ref)
        live = live_length(order_ref, assignment_ref, lengths_ref, which, chunk)
        cot = cot_ref[...]
        masked = jnp.where(rows_below(cot.shape, live), cot, jnp.zeros_like(cot))
        act = act_ref[...]
        gate_acc[...] += contract(act, grad_gate)
        up_acc[...] += contract(act, grad_up)
        down_acc[...] += contract(hidden, masked)

    @pl.when(step == pl.num_programs(0) - 1)
    def _():
        gate_ref[...] = (gate_acc[...] * scale).T.astype(jnp.bfloat16)
        up_ref[...] = (up_acc[...] * scale).T.astype(jnp.bfloat16)
        f_half = down_ref.shape[0]
        first = pl.multiple_of(order_ref[0] * f_half, f_half)
        down_ref[...] = (down_acc[pl.ds(first, f_half), :] * scale).astype(jnp.bfloat16)


def weight_grads(scale, scalars, head_own, head_away, saved, cot, rest):
    rows, lanes = 2 * head_away[0].shape[1], head_away[0].shape[2]
    tok, width = cot.shape
    ffw, half = saved.shape[-1] // 2, width // 2
    column = lambda cols, index: pl.BlockSpec(
        (rows, cols), lambda i, order, *_: (order[2 + i], index)
    )
    out = lambda *shape: pl.BlockSpec(shape, lambda i, *_: (0, 0))
    shape = lambda *dims: jax.ShapeDtypeStruct(dims, jnp.bfloat16)
    return pl.pallas_call(
        functools.partial(weight_kernel, scale),
        grid_spec=pltpu.PrefetchScalarGridSpec(
            num_scalar_prefetch=3,
            grid=(N_X,),
            in_specs=[whole(part) for part in head_own + head_away]
            + [saved_block(saved, 0), saved_block(saved, 1)]
            + [column(half, 3), column(half, 2), column(width, 0), column(width, 0)],
            out_specs=[out(ffw, half), out(ffw, half), out(ffw // 2, width)],
            scratch_shapes=[
                pltpu.VMEM((half, ffw), jnp.float32),
                pltpu.VMEM((half, ffw), jnp.float32),
                pltpu.VMEM((ffw, width), jnp.float32),
                pltpu.VMEM((rows, lanes), jnp.bfloat16),
                pltpu.VMEM((rows, lanes), jnp.bfloat16),
            ],
        ),
        out_shape=[shape(ffw, half), shape(ffw, half), shape(ffw // 2, width)],
        name="weight_grads",
        cost_estimate=pl.CostEstimate(
            flops=8 * tok * ffw * width,
            bytes_accessed=2 * (6 * tok * ffw + cot.size + rest.size),
            transcendentals=2 * tok * ffw,
        ),
    )(*scalars, *head_own, *head_away, saved, saved, rest, rest, cot, rest)


def gather_x(block):
    left, right = shift(block, "x", N_X, 1), shift(block, "x", N_X, -1)
    far_low, far_high = shift(left[0], "x", N_X, 1), shift(right[1], "x", N_X, -1)
    return block, left, right, far_low, far_high


def on_device(
    activations, cotangent, gate_saved, up_saved, w_gate, w_up, w_down, assignment, pair_lengths
):
    batch, x = lax.axis_index("dp"), lax.axis_index("x")
    away = 1 - batch
    rows, width = cotangent.shape
    half = width // 2
    own, ffw = gate_saved.shape
    lanes = -(-ffw // 128) * 128
    row_axes = ("y", "core")
    n_row = N_Y * N_CORE
    tok = rows * n_row
    n_dp = 2
    order = jnp.stack([batch, away] + [(x + step) % N_X for step in (0, N_X - 1, 1, 2)])
    order = order.astype(jnp.int32)
    scalars = (order, assignment, pair_lengths)

    def pick(value, index):
        return lax.dynamic_index_in_dim(value, index, 0, keepdims=False)

    act_own = lax.dynamic_slice_in_dim(activations, batch * half, half, 1)
    act_other = lax.dynamic_slice_in_dim(activations, away * half, half, 1)
    partner = shift(jnp.concatenate([cotangent, act_other], axis=1), "dp", n_dp, 1)

    saved = pack_pair(gate_saved, up_saved)[None]
    saved = lax.all_gather(saved, ("x", "dp", "z"), axis=0, tiled=True)
    saved = saved.reshape(N_X, n_dp, N_Z, own, 2 * ffw)

    cot_own = spread(cotangent, row_axes, n_row).reshape(tok, width)
    block_term = head_term(scalars, cot_own, w_down, lanes)
    head_x = sum_over(block_term.reshape(tok, lanes), "x", N_X)
    _, partner = lax.optimization_barrier((head_x, partner))
    rest = spread(jnp.concatenate([partner, act_own], axis=1), row_axes, n_row)
    rest = rest.reshape(tok, 2 * width)

    head = sum_over(head_x, "z", N_Z)
    head = lax.all_gather(head, ("dp", "z"), axis=0, tiled=True)
    head = head.reshape(n_dp, N_Z * own, lanes)
    halves = (2, N_Z * own // 2, lanes)
    head_own = gather_x(pick(head, batch).reshape(halves))
    head_away = gather_x(pick(head, away).reshape(halves))

    term = input_term(order, head_own, saved, w_gate.T, w_up.T)
    input_grad = sum_over(term, row_axes, n_row)

    scale = 1.0 / math.sqrt(n_dp * tok)
    gate_grad, up_grad, down_grad = weight_grads(
        scale, scalars, head_own, head_away, saved, cot_own, rest
    )
    return input_grad, gate_grad.T, up_grad.T, down_grad


def solution(mesh):
    fine = Mesh(
        mesh.devices.reshape(2, N_Y, N_CORE, N_X, N_Z), ("dp", "y", "core", "x", "z")
    )
    row, col = ("y", "core"), ("x", "z")

    return jax.shard_map(
        on_device,
        mesh=fine,
        in_specs=(
            P(("dp",) + row, col),
            P(("dp",) + row, col),
            P(("dp",) + col, row),
            P(("dp",) + col, row),
            P(col, row),
            P(col, row),
            P(row, col),
            P(),
            P(),
        ),
        out_specs=(
            P(("dp",) + row, col),
            P(col + ("dp",), row),
            P(col + ("dp",), row),
            P(row + ("dp",), col),
        ),
        check_vma=False,
    )
```

```python
import functools
import math
import jax
import jax.numpy as jnp
from jax import lax
from jax.experimental import pallas as pl
from jax.experimental.pallas import tpu as pltpu
from jax.sharding import Mesh, PartitionSpec as P

N_Y, N_CORE, N_X, N_Z = 4, 2, 4, 8


def shift(value, axis, size, step):
    return lax.ppermute(value, axis, [(i, (i + step) % size) for i in range(size)])


def spread(value, axis, size):
    copies = jnp.broadcast_to(value[None], (size,) + value.shape)
    return lax.all_to_all(copies, axis, split_axis=0, concat_axis=0, tiled=True)


def sum_over(value, axis, size):
    blocks = value.reshape(size, value.shape[0] // size, value.shape[1])
    received = lax.all_to_all(blocks, axis, split_axis=0, concat_axis=0, tiled=True)
    return jnp.sum(received, axis=0, dtype=jnp.float32).astype(jnp.bfloat16)


def live_length(order_ref, assignment_ref, lengths_ref, which, chunk):
    slot = 2 * order_ref[which] + lax.div(chunk, 2)
    return lengths_ref[2 * assignment_ref[slot] + lax.rem(chunk, 2)]


def rows_below(shape, count):
    return lax.broadcasted_iota(jnp.int32, shape, 0) < count


def head_kernel(order_ref, assignment_ref, lengths_ref, cot_ref, w_ref, out_ref):
    ffw = w_ref.shape[0]
    chunks, rows, lanes = out_ref.shape
    w_turned = w_ref[...].T
    for chunk in range(chunks):
        live = live_length(order_ref, assignment_ref, lengths_ref, 0, jnp.int32(chunk))
        cot = cot_ref[chunk * rows : (chunk + 1) * rows, :]
        masked = jnp.where(rows_below(cot.shape, live), cot, jnp.zeros_like(cot))
        term = jnp.dot(masked, w_turned, preferred_element_type=jnp.float32)
        out_ref[chunk, :, :ffw] = term.astype(jnp.bfloat16)
        out_ref[chunk, :, ffw:] = jnp.zeros((rows, lanes - ffw), jnp.bfloat16)


def head_term(scalars, cot, w_down, lanes):
    tok, width = cot.shape
    ffw = w_down.shape[0]
    return pl.pallas_call(
        head_kernel,
        in_specs=[pl.BlockSpec(memory_space=pltpu.SMEM)] * 3
        + [pl.BlockSpec(memory_space=pltpu.VMEM)] * 2,
        out_specs=pl.BlockSpec(memory_space=pltpu.VMEM),
        out_shape=jax.ShapeDtypeStruct((N_X, tok // N_X, lanes), jnp.bfloat16),
        name="head_term",
        cost_estimate=pl.CostEstimate(
            flops=2 * tok * width * ffw,
            bytes_accessed=2 * (cot.size + w_down.size + tok * lanes),
            transcendentals=0,
        ),
    )(*scalars, cot, w_down)


def take_part(step, parts, head_ref):
    mid = parts[0].shape[1]
    for index, part in enumerate(parts):
        @pl.when(step == index)
        def _(part=part):
            head_ref[:mid, :] = part[0]
            head_ref[mid:, :] = part[1]


def whole(value):
    return pl.BlockSpec(value.shape, lambda i, *_: (0,) * value.ndim)


def saved_block(saved, which):
    return pl.BlockSpec(
        (1, 1) + saved.shape[2:], lambda i, order, *_: (order[2 + i], order[which], 0, 0, 0)
    )


def pack_kernel(gate_ref, up_ref, out_ref):
    ffw = gate_ref.shape[1]
    body = ffw // 128 * 128
    out_ref[:, :body] = gate_ref[:, :body]
    out_ref[:, body : 2 * body] = up_ref[:, :body]
    out_ref[:, 2 * body : body + ffw] = gate_ref[:, body:]
    out_ref[:, body + ffw :] = up_ref[:, body:]


def pack_pair(gate, up):
    shape = jax.ShapeDtypeStruct((gate.shape[0], 2 * gate.shape[1]), gate.dtype)
    return pl.pallas_call(pack_kernel, out_shape=shape, name="pack_pair")(gate, up)


def swiglu_terms(saved_ref):
    pair = saved_ref[0, 0]
    pair = pair.reshape(pair.shape[0] * pair.shape[1], pair.shape[2]).astype(jnp.float32)
    ffw = pair.shape[1] // 2
    body = ffw // 128 * 128
    tail = pair[:, 2 * body :]
    turned = pltpu.roll(tail, ffw - body, 1)
    gate = jnp.concatenate([pair[:, :body], tail[:, : ffw - body]], axis=1)
    up = jnp.concatenate([pair[:, body : 2 * body], turned[:, : ffw - body]], axis=1)
    sig = 0.5 * jnp.tanh(0.5 * gate) + 0.5
    silu = gate * sig
    return up, silu, up * (sig + silu * (1.0 - sig))


def gradients(head_ref, saved_ref):
    up, silu, slope = swiglu_terms(saved_ref)
    head = head_ref[:, : up.shape[1]].astype(jnp.float32)
    return (
        (head * slope).astype(jnp.bfloat16),
        (head * silu).astype(jnp.bfloat16),
        (silu * up).astype(jnp.bfloat16),
    )


def input_kernel(
    order_ref, here, left, right, far, saved_ref, w_gate_ref, w_up_ref,
    out_ref, head_ref,
):
    take_part(pl.program_id(0), (here, left, right, far), head_ref)
    grad_gate, grad_up, _ = gradients(head_ref, saved_ref)
    term = jnp.dot(grad_gate, w_gate_ref[...], preferred_element_type=jnp.float32)
    term += jnp.dot(grad_up, w_up_ref[...], preferred_element_type=jnp.float32)
    out_ref[...] = term.astype(jnp.bfloat16)


def input_term(order, head, saved, w_gate, w_up):
    rows, lanes = 2 * head[0].shape[1], head[0].shape[2]
    ffw, width = w_gate.shape
    tok = N_X * rows
    return pl.pallas_call(
        input_kernel,
        grid_spec=pltpu.PrefetchScalarGridSpec(
            num_scalar_prefetch=1,
            grid=(N_X,),
            in_specs=[whole(part) for part in head]
            + [saved_block(saved, 0), whole(w_gate), whole(w_up)],
            out_specs=pl.BlockSpec((rows, width), lambda i, order: (order[2 + i], 0)),
            scratch_shapes=[pltpu.VMEM((rows, lanes), jnp.bfloat16)],
        ),
        out_shape=jax.ShapeDtypeStruct((tok, width), jnp.bfloat16),
        name="input_term",
        cost_estimate=pl.CostEstimate(
            flops=4 * tok * ffw * width,
            bytes_accessed=2 * (3 * tok * ffw + 2 * w_gate.size + tok * width),
            transcendentals=tok * ffw,
        ),
    )(order, *head, saved, w_gate, w_up)


def weight_kernel(
    scale, order_ref, assignment_ref, lengths_ref,
    *refs,
):
    parts_own, parts_away, refs = refs[:4], refs[4:8], refs[8:]
    saved_own, saved_away, act_own, act_away, cot_own, cot_away = refs[:6]
    gate_ref, up_ref, down_ref, gate_acc, up_acc, down_acc, head_own, head_away = refs[6:]
    step = pl.program_id(0)
    chunk = order_ref[2 + step]

    @pl.when(step == 0)
    def _():
        gate_acc[...] = jnp.zeros_like(gate_acc)
        up_acc[...] = jnp.zeros_like(up_acc)
        down_acc[...] = jnp.zeros_like(down_acc)

    def contract(left_rows, right_rows):
        return lax.dot_general(
            left_rows, right_rows, (((0,), (0,)), ((), ())), preferred_element_type=jnp.float32
        )

    take_part(step, parts_own, head_own)
    take_part(step, parts_away, head_away)
    for which, head_ref, saved_ref, act_ref, cot_ref in (
        (0, head_own, saved_own, act_own, cot_own),
        (1, head_away, saved_away, act_away, cot_away),
    ):
        grad_gate, grad_up, hidden = gradients(head_ref, saved_ref)
        live = live_length(order_ref, assignment_ref, lengths_ref, which, chunk)
        cot = cot_ref[...]
        masked = jnp.where(rows_below(cot.shape, live), cot, jnp.zeros_like(cot))
        act = act_ref[...]
        gate_acc[...] += contract(act, grad_gate)
        up_acc[...] += contract(act, grad_up)
        down_acc[...] += contract(hidden, masked)

    @pl.when(step == pl.num_programs(0) - 1)
    def _():
        gate_ref[...] = (gate_acc[...] * scale).T.astype(jnp.bfloat16)
        up_ref[...] = (up_acc[...] * scale).T.astype(jnp.bfloat16)
        f_half = down_ref.shape[0]
        first = pl.multiple_of(order_ref[0] * f_half, f_half)
        down_ref[...] = (down_acc[pl.ds(first, f_half), :] * scale).astype(jnp.bfloat16)


def weight_grads(scale, scalars, head_own, head_away, saved, cot, rest):
    rows, lanes = 2 * head_away[0].shape[1], head_away[0].shape[2]
    tok, width = cot.shape
    ffw, half = saved.shape[-1] // 2, width // 2
    column = lambda cols, index: pl.BlockSpec(
        (rows, cols), lambda i, order, *_: (order[2 + i], index)
    )
    out = lambda *shape: pl.BlockSpec(shape, lambda i, *_: (0, 0))
    shape = lambda *dims: jax.ShapeDtypeStruct(dims, jnp.bfloat16)
    return pl.pallas_call(
        functools.partial(weight_kernel, scale),
        grid_spec=pltpu.PrefetchScalarGridSpec(
            num_scalar_prefetch=3,
            grid=(N_X,),
            in_specs=[whole(part) for part in head_own + head_away]
            + [saved_block(saved, 0), saved_block(saved, 1)]
            + [column(half, 3), column(half, 2), column(width, 0), column(width, 0)],
            out_specs=[out(ffw, half), out(ffw, half), out(ffw // 2, width)],
            scratch_shapes=[
                pltpu.VMEM((half, ffw), jnp.float32),
                pltpu.VMEM((half, ffw), jnp.float32),
                pltpu.VMEM((ffw, width), jnp.float32),
                pltpu.VMEM((rows, lanes), jnp.bfloat16),
                pltpu.VMEM((rows, lanes), jnp.bfloat16),
            ],
        ),
        out_shape=[shape(ffw, half), shape(ffw, half), shape(ffw // 2, width)],
        name="weight_grads",
        cost_estimate=pl.CostEstimate(
            flops=8 * tok * ffw * width,
            bytes_accessed=2 * (6 * tok * ffw + cot.size + rest.size),
            transcendentals=2 * tok * ffw,
        ),
    )(*scalars, *head_own, *head_away, saved, saved, rest, rest, cot, rest)


def gather_x(block, onward):
    left = shift(block, "x", N_X, 1)
    right = shift(block, "x", N_X, -1)
    far = shift(left if onward == 1 else right, "x", N_X, onward)
    return block, left, right, far


def on_device(
    activations, cotangent, gate_saved, up_saved, w_gate, w_up, w_down, assignment, pair_lengths
):
    batch, x = lax.axis_index("dp"), lax.axis_index("x")
    away = 1 - batch
    rows, width = cotangent.shape
    half = width // 2
    own, ffw = gate_saved.shape
    lanes = -(-ffw // 128) * 128
    row_axes = ("y", "core")
    n_row = N_Y * N_CORE
    tok = rows * n_row
    n_dp = 2
    order = jnp.stack([batch, away] + [(x + step) % N_X for step in (0, N_X - 1, 1, 2)])
    order = order.astype(jnp.int32)
    scalars = (order, assignment, pair_lengths)

    def pick(value, index):
        return lax.dynamic_index_in_dim(value, index, 0, keepdims=False)

    act_own = lax.dynamic_slice_in_dim(activations, batch * half, half, 1)
    act_other = lax.dynamic_slice_in_dim(activations, away * half, half, 1)
    partner = shift(jnp.concatenate([cotangent, act_other], axis=1), "dp", n_dp, 1)

    saved = pack_pair(gate_saved, up_saved)[None]
    saved = lax.all_gather(saved, ("x", "dp", "z"), axis=0, tiled=True)
    saved = saved.reshape(N_X, n_dp, N_Z, own, 2 * ffw)

    cot_own = spread(cotangent, row_axes, n_row).reshape(tok, width)
    block_term = head_term(scalars, cot_own, w_down, lanes)
    head_x = sum_over(block_term.reshape(tok, lanes), "x", N_X)
    _, partner = lax.optimization_barrier((head_x, partner))
    rest = spread(jnp.concatenate([partner, act_own], axis=1), row_axes, n_row)
    rest = rest.reshape(tok, 2 * width)

    head = sum_over(head_x, "z", N_Z)
    head = lax.all_gather(head, ("dp", "z"), axis=0, tiled=True)
    head = head.reshape(n_dp, N_Z * own, lanes)
    halves = (2, N_Z * own // 2, lanes)
    head_own = gather_x(pick(head, batch).reshape(halves), 1)
    head_away = gather_x(pick(head, away).reshape(halves), -1)

    term = input_term(order, head_own, saved, w_gate.T, w_up.T)
    input_grad = sum_over(term, row_axes, n_row)

    scale = 1.0 / math.sqrt(n_dp * tok)
    gate_grad, up_grad, down_grad = weight_grads(
        scale, scalars, head_own, head_away, saved, cot_own, rest
    )
    return input_grad, gate_grad.T, up_grad.T, down_grad


def solution(mesh):
    fine = Mesh(
        mesh.devices.reshape(2, N_Y, N_CORE, N_X, N_Z), ("dp", "y", "core", "x", "z")
    )
    row, col = ("y", "core"), ("x", "z")

    return jax.shard_map(
        on_device,
        mesh=fine,
        in_specs=(
            P(("dp",) + row, col),
            P(("dp",) + row, col),
            P(("dp",) + col, row),
            P(("dp",) + col, row),
            P(col, row),
            P(col, row),
            P(row, col),
            P(),
            P(),
        ),
        out_specs=(
            P(("dp",) + row, col),
            P(col + ("dp",), row),
            P(col + ("dp",), row),
            P(row + ("dp",), col),
        ),
        check_vma=False,
    )
```

```python
import functools
import math
import jax
import jax.numpy as jnp
from jax import lax
from jax.experimental import pallas as pl
from jax.experimental.pallas import tpu as pltpu
from jax.sharding import Mesh, PartitionSpec as P

N_Y, N_CORE, N_X, N_Z = 4, 2, 4, 8


def shift(value, axis, size, step):
    return lax.ppermute(value, axis, [(i, (i + step) % size) for i in range(size)])


def spread(value, axis, size):
    copies = jnp.broadcast_to(value[None], (size,) + value.shape)
    return lax.all_to_all(copies, axis, split_axis=0, concat_axis=0, tiled=True)


def sum_over(value, axis, size):
    blocks = value.reshape(size, value.shape[0] // size, value.shape[1])
    received = lax.all_to_all(blocks, axis, split_axis=0, concat_axis=0, tiled=True)
    return jnp.sum(received, axis=0, dtype=jnp.float32).astype(jnp.bfloat16)


def live_length(order_ref, assignment_ref, lengths_ref, which, chunk):
    slot = 2 * order_ref[which] + lax.div(chunk, 2)
    return lengths_ref[2 * assignment_ref[slot] + lax.rem(chunk, 2)]


def rows_below(shape, count):
    return lax.broadcasted_iota(jnp.int32, shape, 0) < count


def head_kernel(order_ref, assignment_ref, lengths_ref, cot_ref, w_ref, out_ref):
    ffw = w_ref.shape[0]
    chunks, rows, lanes = out_ref.shape
    w_turned = w_ref[...].T
    for chunk in range(chunks):
        live = live_length(order_ref, assignment_ref, lengths_ref, 0, jnp.int32(chunk))
        cot = cot_ref[chunk * rows : (chunk + 1) * rows, :]
        masked = jnp.where(rows_below(cot.shape, live), cot, jnp.zeros_like(cot))
        term = jnp.dot(masked, w_turned, preferred_element_type=jnp.float32)
        out_ref[chunk, :, :ffw] = term.astype(jnp.bfloat16)
        out_ref[chunk, :, ffw:] = jnp.zeros((rows, lanes - ffw), jnp.bfloat16)


def head_term(scalars, cot, w_down, lanes):
    tok, width = cot.shape
    ffw = w_down.shape[0]
    return pl.pallas_call(
        head_kernel,
        in_specs=[pl.BlockSpec(memory_space=pltpu.SMEM)] * 3
        + [pl.BlockSpec(memory_space=pltpu.VMEM)] * 2,
        out_specs=pl.BlockSpec(memory_space=pltpu.VMEM),
        out_shape=jax.ShapeDtypeStruct((N_X, tok // N_X, lanes), jnp.bfloat16),
        name="head_term",
        cost_estimate=pl.CostEstimate(
            flops=2 * tok * width * ffw,
            bytes_accessed=2 * (cot.size + w_down.size + tok * lanes),
            transcendentals=0,
        ),
    )(*scalars, cot, w_down)


def take_part(step, parts, head_ref):
    here, left, right, far_low, far_high = parts
    mid = far_low.shape[0]
    for index, part in enumerate((here, left, right)):
        @pl.when(step == index)
        def _(part=part):
            head_ref[:mid, :] = part[0]
            head_ref[mid:, :] = part[1]

    @pl.when(step == 3)
    def _():
        head_ref[:mid, :] = far_low[...]
        head_ref[mid:, :] = far_high[...]


def whole(value):
    return pl.BlockSpec(value.shape, lambda i, *_: (0,) * value.ndim)


def saved_block(saved, which):
    return pl.BlockSpec(
        (1, saved.shape[1], 1) + saved.shape[3:],
        lambda i, order, *_: (order[which], 0, order[2 + i], 0, 0),
    )


def pack_kernel(gate_ref, up_ref, out_ref):
    ffw = gate_ref.shape[1]
    body = ffw // 128 * 128
    out_ref[:, :body] = gate_ref[:, :body]
    out_ref[:, body : 2 * body] = up_ref[:, :body]
    out_ref[:, 2 * body : body + ffw] = gate_ref[:, body:]
    out_ref[:, body + ffw :] = up_ref[:, body:]


def pack_pair(gate, up):
    shape = jax.ShapeDtypeStruct((gate.shape[0], 2 * gate.shape[1]), gate.dtype)
    return pl.pallas_call(pack_kernel, out_shape=shape, name="pack_pair")(gate, up)


def swiglu_terms(saved_ref):
    pair = saved_ref[0, :, 0]
    pair = pair.reshape(pair.shape[0] * pair.shape[1], pair.shape[2]).astype(jnp.float32)
    ffw = pair.shape[1] // 2
    body = ffw // 128 * 128
    tail = pair[:, 2 * body :]
    turned = pltpu.roll(tail, ffw - body, 1)
    gate = jnp.concatenate([pair[:, :body], tail[:, : ffw - body]], axis=1)
    up = jnp.concatenate([pair[:, body : 2 * body], turned[:, : ffw - body]], axis=1)
    sig = jax.nn.sigmoid(gate)
    silu = gate * sig
    return up, silu, up * sig * (1.0 + gate * (1.0 - sig))


def gradients(head_ref, saved_ref):
    up, silu, slope = swiglu_terms(saved_ref)
    head = head_ref[:, : up.shape[1]].astype(jnp.float32)
    return (
        (head * slope).astype(jnp.bfloat16),
        (head * silu).astype(jnp.bfloat16),
        (silu * up).astype(jnp.bfloat16),
    )


def input_kernel(
    order_ref, here, left, right, far_low, far_high, saved_ref, w_gate_ref, w_up_ref,
    out_ref, head_ref,
):
    take_part(pl.program_id(0), (here, left, right, far_low, far_high), head_ref)
    grad_gate, grad_up, _ = gradients(head_ref, saved_ref)
    term = jnp.dot(grad_gate, w_gate_ref[...], preferred_element_type=jnp.float32)
    term += jnp.dot(grad_up, w_up_ref[...], preferred_element_type=jnp.float32)
    out_ref[...] = term.astype(jnp.bfloat16)


def input_term(order, head, saved, w_gate, w_up):
    rows, lanes = 2 * head[0].shape[1], head[0].shape[2]
    ffw, width = w_gate.shape
    tok = N_X * rows
    return pl.pallas_call(
        input_kernel,
        grid_spec=pltpu.PrefetchScalarGridSpec(
            num_scalar_prefetch=1,
            grid=(N_X,),
            in_specs=[whole(part) for part in head]
            + [saved_block(saved, 0), whole(w_gate), whole(w_up)],
            out_specs=pl.BlockSpec((rows, width), lambda i, order: (order[2 + i], 0)),
            scratch_shapes=[pltpu.VMEM((rows, lanes), jnp.bfloat16)],
        ),
        out_shape=jax.ShapeDtypeStruct((tok, width), jnp.bfloat16),
        name="input_term",
        cost_estimate=pl.CostEstimate(
            flops=4 * tok * ffw * width,
            bytes_accessed=2 * (3 * tok * ffw + 2 * w_gate.size + tok * width),
            transcendentals=tok * ffw,
        ),
    )(order, *head, saved, w_gate, w_up)


def weight_kernel(
    scale, order_ref, assignment_ref, lengths_ref,
    *refs,
):
    parts_own, parts_away, refs = refs[:5], refs[5:10], refs[10:]
    saved_own, saved_away, act_own, act_away, cot_own, cot_away = refs[:6]
    gate_ref, up_ref, down_ref, gate_acc, up_acc, down_acc, head_own, head_away = refs[6:]
    step = pl.program_id(0)
    chunk = order_ref[2 + step]

    @pl.when(step == 0)
    def _():
        gate_acc[...] = jnp.zeros_like(gate_acc)
        up_acc[...] = jnp.zeros_like(up_acc)
        down_acc[...] = jnp.zeros_like(down_acc)

    def contract(left_rows, right_rows):
        return lax.dot_general(
            left_rows, right_rows, (((0,), (0,)), ((), ())), preferred_element_type=jnp.float32
        )

    take_part(step, parts_own, head_own)
    take_part(step, parts_away, head_away)
    for which, head_ref, saved_ref, act_ref, cot_ref in (
        (0, head_own, saved_own, act_own, cot_own),
        (1, head_away, saved_away, act_away, cot_away),
    ):
        grad_gate, grad_up, hidden = gradients(head_ref, saved_ref)
        live = live_length(order_ref, assignment_ref, lengths_ref, which, chunk)
        cot = cot_ref[...]
        masked = jnp.where(rows_below(cot.shape, live), cot, jnp.zeros_like(cot))
        act = act_ref[...]
        gate_acc[...] += contract(act, grad_gate)
        up_acc[...] += contract(act, grad_up)
        down_acc[...] += contract(hidden, masked)

    @pl.when(step == pl.num_programs(0) - 1)
    def _():
        gate_ref[...] = (gate_acc[...] * scale).T.astype(jnp.bfloat16)
        up_ref[...] = (up_acc[...] * scale).T.astype(jnp.bfloat16)
        f_half = down_ref.shape[0]
        first = pl.multiple_of(order_ref[0] * f_half, f_half)
        down_ref[...] = (down_acc[pl.ds(first, f_half), :] * scale).astype(jnp.bfloat16)


def weight_grads(scale, scalars, head_own, head_away, saved, cot, rest):
    rows, lanes = 2 * head_away[0].shape[1], head_away[0].shape[2]
    tok, width = cot.shape
    ffw, half = saved.shape[-1] // 2, width // 2
    column = lambda cols, index: pl.BlockSpec(
        (rows, cols), lambda i, order, *_: (order[2 + i], index)
    )
    out = lambda *shape: pl.BlockSpec(shape, lambda i, *_: (0, 0))
    shape = lambda *dims: jax.ShapeDtypeStruct(dims, jnp.bfloat16)
    return pl.pallas_call(
        functools.partial(weight_kernel, scale),
        grid_spec=pltpu.PrefetchScalarGridSpec(
            num_scalar_prefetch=3,
            grid=(N_X,),
            in_specs=[whole(part) for part in head_own + head_away]
            + [saved_block(saved, 0), saved_block(saved, 1)]
            + [column(half, 3), column(half, 2), column(width, 0), column(width, 0)],
            out_specs=[out(ffw, half), out(ffw, half), out(ffw // 2, width)],
            scratch_shapes=[
                pltpu.VMEM((half, ffw), jnp.float32),
                pltpu.VMEM((half, ffw), jnp.float32),
                pltpu.VMEM((ffw, width), jnp.float32),
                pltpu.VMEM((rows, lanes), jnp.bfloat16),
                pltpu.VMEM((rows, lanes), jnp.bfloat16),
            ],
        ),
        out_shape=[shape(ffw, half), shape(ffw, half), shape(ffw // 2, width)],
        name="weight_grads",
        cost_estimate=pl.CostEstimate(
            flops=8 * tok * ffw * width,
            bytes_accessed=2 * (6 * tok * ffw + cot.size + rest.size),
            transcendentals=2 * tok * ffw,
        ),
    )(*scalars, *head_own, *head_away, saved, saved, rest, rest, cot, rest)


def gather_x(block):
    left, right = shift(block, "x", N_X, 1), shift(block, "x", N_X, -1)
    far_low, far_high = shift(left[0], "x", N_X, 1), shift(right[1], "x", N_X, -1)
    return block, left, right, far_low, far_high


def on_device(
    activations, cotangent, gate_saved, up_saved, w_gate, w_up, w_down, assignment, pair_lengths
):
    batch, x = lax.axis_index("dp"), lax.axis_index("x")
    away = 1 - batch
    rows, width = cotangent.shape
    half = width // 2
    own, ffw = gate_saved.shape
    lanes = -(-ffw // 128) * 128
    row_axes = ("y", "core")
    n_row = N_Y * N_CORE
    tok = rows * n_row
    n_dp = 2
    order = jnp.stack([batch, away] + [(x + step) % N_X for step in (0, N_X - 1, 1, 2)])
    order = order.astype(jnp.int32)
    scalars = (order, assignment, pair_lengths)

    def pick(value, index):
        return lax.dynamic_index_in_dim(value, index, 0, keepdims=False)

    act_own = lax.dynamic_slice_in_dim(activations, batch * half, half, 1)
    act_other = lax.dynamic_slice_in_dim(activations, away * half, half, 1)
    partner = shift(jnp.concatenate([cotangent, act_other], axis=1), "dp", n_dp, 1)

    saved = pack_pair(gate_saved, up_saved)[None]
    saved = lax.all_gather(saved, ("dp", "z", "x"), axis=0, tiled=True)
    saved = saved.reshape(n_dp, N_Z, N_X, own, 2 * ffw)

    cot_own = spread(cotangent, row_axes, n_row).reshape(tok, width)
    block_term = head_term(scalars, cot_own, w_down, lanes)
    head_x = sum_over(block_term.reshape(tok, lanes), "x", N_X)
    _, partner = lax.optimization_barrier((head_x, partner))
    rest = spread(jnp.concatenate([partner, act_own], axis=1), row_axes, n_row)
    rest = rest.reshape(tok, 2 * width)

    head = sum_over(head_x, "z", N_Z)
    head = lax.all_gather(head, ("dp", "z"), axis=0, tiled=True)
    head = head.reshape(n_dp, N_Z * own, lanes)
    halves = (2, N_Z * own // 2, lanes)
    head_own = gather_x(pick(head, batch).reshape(halves))
    head_away = gather_x(pick(head, away).reshape(halves))

    term = input_term(order, head_own, saved, w_gate.T, w_up.T)
    input_grad = sum_over(term, row_axes, n_row)

    scale = 1.0 / math.sqrt(n_dp * tok)
    gate_grad, up_grad, down_grad = weight_grads(
        scale, scalars, head_own, head_away, saved, cot_own, rest
    )
    return input_grad, gate_grad.T, up_grad.T, down_grad


def solution(mesh):
    fine = Mesh(
        mesh.devices.reshape(2, N_Y, N_CORE, N_X, N_Z), ("dp", "y", "core", "x", "z")
    )
    row, col = ("y", "core"), ("x", "z")

    return jax.shard_map(
        on_device,
        mesh=fine,
        in_specs=(
            P(("dp",) + row, col),
            P(("dp",) + row, col),
            P(("dp",) + col, row),
            P(("dp",) + col, row),
            P(col, row),
            P(col, row),
            P(row, col),
            P(),
            P(),
        ),
        out_specs=(
            P(("dp",) + row, col),
            P(col + ("dp",), row),
            P(col + ("dp",), row),
            P(row + ("dp",), col),
        ),
        check_vma=False,
    )
```
